128 devices in a mesh: seq: 16 (over y_lo, x, core), tp: 8 (over y_hi, z).
Axes of the slice: x: 4, y: 4 (y_hi: 2, y_lo: 2; y = y_hi * 2 + y_lo), z: 4, core: 2. Of those that a mesh axis runs over, the one named last changes fastest.
Arguments:
- queries: bfloat16 [8192, 6144], P('seq', 'tp'), may hold values from -6 to 6
- keys: bfloat16 [8192, 1024], P('seq', 'tp'), may hold values from -6 to 6
- values: bfloat16 [8192, 1024], P('seq', 'tp'), may hold values from -6 to 6
- segment_ids: int32 [8192], replicated, may hold values from 0 to 7, never falling along the last dimension, each value on 1 to 6144 neighbouring positions
- packing: int32 [64, 2], replicated, may hold values from 0 to 15, as said below
- out_weight: bfloat16 [6144, 12288], P('tp', 'seq'), may hold values from -0.625 to 0.625
Outputs:
- attended: bfloat16 [8192, 12288], P('seq', 'tp')
The draws below stay inside these ranges and needn't reach their ends.
Inputs may be any that keep to these rules, and one draw needn't show every extreme that they name: `packing`: each arriving block gets a distinct packed place, so every packed shard receives exactly 4 blocks at offsets 0 to 3; the blocks of one shard go to 4 different packed shards. `segment_ids`: document ids never fall along the tokens; each document has 1 to 6144 tokens and one has exactly 6144.
All inputs are finite; a program needn't handle non-finite values.
Results may differ from the reference program's by a relative error of at most 0.015.
Values may be sent and summed in bfloat16 or wider, within the bound.
A program may use at most 128 MiB of HBM per device.

```python
import math
import jax
import jax.numpy as jnp
import numpy as np
from jax import lax

D = 12288
HEAD_DIM = 128
KV_HEADS = 8
HEADS = 48
WINDOW = 4096
BLOCK = 128
TOK_DEV = 512
TOKENS = 8192
HD = 6144
KVD = 1024
BPD = 4
NBLK = 64
DOCS = 8
DOC_MOST = 6144
N_TP = 8


def draw_queries(key, part):
    base = jnp.clip(1.41 * jax.random.normal(jax.random.fold_in(key, 1), (TOKENS, HD), jnp.float32), -6.0, 6.0)
    return base.astype(jnp.bfloat16)


def draw_keys(key, part):
    base = jnp.clip(1.41 * jax.random.normal(jax.random.fold_in(key, 2), (TOKENS, KVD), jnp.float32), -6.0, 6.0)
    return base.astype(jnp.bfloat16)


def draw_packing(key, part):
    shard_count = NBLK // BPD
    key_place, key_shift, key_order, key_offset = jax.random.split(jax.random.fold_in(key, 11), 4)
    placed = jax.random.permutation(key_place, shard_count).astype(jnp.int32)
    shifts = jax.random.permutation(key_shift, shard_count)[:BPD].astype(jnp.int32)
    tie_break = jnp.arange(BPD, dtype=jnp.int32)[None, :]
    slot_order = jnp.argsort(jax.random.randint(key_order, (shard_count, BPD), 0, 4096) * BPD + tie_break, axis=1).astype(jnp.int32)
    target_shard = (placed[:, None] + shifts[slot_order]) % shard_count
    offset_table = jnp.argsort(jax.random.randint(key_offset, (shard_count, BPD), 0, 4096) * BPD + tie_break, axis=1).astype(jnp.int32)
    target_offset = offset_table[target_shard, slot_order]
    return jnp.stack([target_shard.reshape(-1), target_offset.reshape(-1)], axis=1).astype(jnp.int32)


def raised(values, key, source, target, shards_of, factor):
    def block_of(dim):
        return (jnp.arange(values.shape[dim]) // (values.shape[dim] // shards_of)).reshape((-1,) + (1,) * (values.ndim - 1 - dim))

    first = jax.random.permutation(key, shards_of)[block_of(target)]
    second = (block_of(target) + shards_of // 2) % shards_of
    return jnp.where((block_of(source) == first) | (block_of(source) == second), factor * values, values)


def shard_levels(stream_key, shape, cuts, smallest, top_value):
    factor_of, own = 1.0, jax.random.fold_in(stream_key, 6)
    for dim, shards_of in cuts:
        steps = jnp.exp(jax.random.uniform(jax.random.fold_in(own, dim), (shards_of,), jnp.float32, smallest / len(cuts), top_value / len(cuts)))
        factor_of = factor_of * jnp.repeat(steps, shape[dim] // shards_of).reshape([-1 if axis == dim else 1 for axis in range(len(shape))])
    return factor_of


def profile(count, total, bound, slope):
    portions = [(1 << 20) // math.isqrt(standing ** slope) + 1 for standing in range(2, count + 1)]
    spare, counts = total - bound - (count - 1), [1] * (count - 1)
    while spare > 0:
        movable = [i for i in range(count - 1) if counts[i] < bound]
        pool, budget = sum([portions[i] for i in movable]), spare
        for i in movable:
            extra = min(bound - counts[i], max(1, budget * portions[i] // pool), spare)
            counts[i] = counts[i] + extra
            spare = spare - extra
    return np.array([bound] + counts)


def ragged_sizes(stream_key, number_of, total, bound, skew):
    if number_of == 2:
        one = jax.random.randint(stream_key, (), max(1, total - bound), min(bound, total - 1) + 1)
        return jnp.stack([one, total - one])
    lengths = jnp.asarray(profile(number_of, total, bound, skew), jnp.int32)
    twos = (number_of - 1) // 2
    giver, taker = lengths[1:1 + 2 * twos:2], lengths[2:2 + 2 * twos:2]
    margin = jnp.minimum(giver - 1, bound - taker)
    moved = jax.random.randint(jax.random.fold_in(stream_key, 1), (twos,), 0, 1 << 20) % (margin + 1)
    lengths = lengths.at[1:1 + 2 * twos:2].set(giver - moved).at[2:2 + 2 * twos:2].set(taker + moved)
    return lengths[jax.random.permutation(jax.random.fold_in(stream_key, 2), number_of)]


def scatter_about(rng, dims, scale, reach, cuts=(), kind=jnp.bfloat16):
    values = scale * jax.random.normal(rng, dims, jnp.float32)
    if cuts:
        values = values * shard_levels(rng, dims, cuts, -0.22, 0.18)
    return jnp.clip(values, -reach, reach).astype(kind)


def noise_with(stream_key, dims, width, bound, shards, heavy, held_as=jnp.bfloat16):
    entries = width * jax.random.normal(stream_key, dims, jnp.float32)
    if shards:
        entries = entries * shard_levels(stream_key, dims, shards, -0.22, 0.18)
    return jnp.clip(raised(entries, jax.random.fold_in(stream_key, 3), *heavy), -bound, bound).astype(held_as)


def setup_inputs(seed: int = 0) -> dict:
    streams_of = jax.random.split(jax.random.key(seed), 7)
    return {
        "queries": draw_queries(jax.random.fold_in(streams_of[6], 71), 0),
        "keys": draw_keys(jax.random.fold_in(streams_of[6], 71), 0),
        "values": scatter_about(streams_of[2], (TOKENS, KVD), 1.0, 6.0, ((0, 16), (1, 8))),
        "segment_ids": jnp.searchsorted(jnp.cumsum(ragged_sizes(streams_of[3], DOCS, TOKENS, DOC_MOST, 2)), jnp.arange(TOKENS), side="right").astype(jnp.int32),
        "packing": draw_packing(jax.random.fold_in(streams_of[6], 71), 0),
        "out_weight": noise_with(streams_of[5], (HD, D), (HD // 32) ** -0.5, 0.625, ((0, 8), (1, 16)), (0, 1, 16, 2.0)),
    }


def attend_head(q_rows, k_rows, v_rows, q_pos, k_pos, q_seg, k_seg):
    scores = lax.dot_general(q_rows, k_rows, (((1,), (1,)), ((), ())), preferred_element_type=jnp.float32)
    scores = scores * (1.0 / math.sqrt(HEAD_DIM))
    allowed = (k_pos[None, :] <= q_pos[:, None]) & (k_pos[None, :] > q_pos[:, None] - WINDOW)
    allowed = allowed & (k_seg[None, :] == q_seg[:, None])
    scores = jnp.where(allowed, scores, -jnp.inf)
    top_score = lax.optimization_barrier(jnp.max(scores, axis=1, keepdims=True))
    expo = jnp.exp(scores - top_score)
    weights = (expo / lax.optimization_barrier(jnp.sum(expo, axis=1, keepdims=True))).astype(jnp.bfloat16)
    return jnp.dot(weights, v_rows, preferred_element_type=jnp.float32).astype(jnp.bfloat16)

def reference(queries, keys, values, segment_ids, packing, out_weight):
    target = packing[:, 0] * BPD + packing[:, 1]
    source = jnp.zeros((NBLK,), jnp.int32).at[target].set(jnp.arange(NBLK, dtype=jnp.int32))

    def repack(array):
        return array.reshape(NBLK, BLOCK, array.shape[1])[source].reshape(TOKENS, array.shape[1])
    packed_q = repack(queries)
    packed_k = repack(keys)
    packed_v = repack(values)
    group_size = HEADS // KV_HEADS
    padded_k = jnp.concatenate([jnp.zeros((WINDOW, KVD), jnp.bfloat16), packed_k], axis=0)
    padded_v = jnp.concatenate([jnp.zeros((WINDOW, KVD), jnp.bfloat16), packed_v], axis=0)
    padded_seg = jnp.concatenate([jnp.full((WINDOW,), -1, jnp.int32), segment_ids], axis=0)

    def one_block(block_index):
        first_row = (block_index * TOK_DEV).astype(jnp.int32)
        q_block = lax.dynamic_slice_in_dim(packed_q, first_row, TOK_DEV, 0)
        k_block = lax.dynamic_slice_in_dim(padded_k, first_row, WINDOW + TOK_DEV, 0)
        v_block = lax.dynamic_slice_in_dim(padded_v, first_row, WINDOW + TOK_DEV, 0)
        q_pos = first_row + jnp.arange(TOK_DEV, dtype=jnp.int32)
        k_pos = first_row - WINDOW + jnp.arange(WINDOW + TOK_DEV, dtype=jnp.int32)
        q_seg = lax.dynamic_slice_in_dim(segment_ids, first_row, TOK_DEV, 0)
        k_seg = lax.dynamic_slice_in_dim(padded_seg, first_row, WINDOW + TOK_DEV, 0)

        def one_head(head_index):
            q_head = lax.dynamic_slice_in_dim(q_block, head_index * HEAD_DIM, HEAD_DIM, 1)
            kv_start = head_index // group_size * HEAD_DIM
            k_head = lax.dynamic_slice_in_dim(k_block, kv_start, HEAD_DIM, 1)
            v_head = lax.dynamic_slice_in_dim(v_block, kv_start, HEAD_DIM, 1)
            return attend_head(q_head, k_head, v_head, q_pos, k_pos, q_seg, k_seg)
        per_head = lax.map(one_head, jnp.arange(HEADS, dtype=jnp.int32))
        return jnp.transpose(per_head, (1, 0, 2)).reshape(TOK_DEV, HD)
    heads_out = lax.map(one_block, jnp.arange(TOKENS // TOK_DEV, dtype=jnp.int32)).reshape(TOKENS, HD)
    group_rows = HD // N_TP

    def add_group(group_index, running):
        first_col = (group_index * group_rows).astype(jnp.int32)
        part_cols = lax.dynamic_slice_in_dim(heads_out, first_col, group_rows, 1)
        part_rows = lax.dynamic_slice_in_dim(out_weight, first_col, group_rows, 0)
        partial_sum = jnp.dot(part_cols, part_rows, preferred_element_type=jnp.float32)
        rounded = lax.optimization_barrier(partial_sum.astype(jnp.bfloat16))
        return running + rounded.astype(jnp.float32)
    total = lax.fori_loop(0, N_TP, add_group, jnp.zeros((TOKENS, D), jnp.float32))
    return total.astype(jnp.bfloat16)
```

```python
import functools
import math

import jax
import jax.numpy as jnp
from jax import lax
from jax.sharding import Mesh, PartitionSpec as P

HEAD_DIM = 128
WINDOW = 4096
BLOCK = 128
SEQ = ("ylo", "x", "c")
TP = ("yhi", "z")


def attend_head(q_rows, k_rows, v_rows, q_pos, k_pos, q_seg, k_seg):
    scores = lax.dot_general(
        q_rows, k_rows, (((1,), (1,)), ((), ())), preferred_element_type=jnp.float32
    )
    scores = scores * (1.0 / math.sqrt(HEAD_DIM))
    allowed = (k_pos[None, :] <= q_pos[:, None]) & (k_pos[None, :] > q_pos[:, None] - WINDOW)
    allowed = allowed & (k_seg[None, :] == q_seg[:, None])
    scores = jnp.where(allowed, scores, -jnp.inf)
    top_score = jnp.max(scores, axis=1, keepdims=True)
    expo = jnp.exp(scores - top_score)
    weights = (expo / jnp.sum(expo, axis=1, keepdims=True)).astype(jnp.bfloat16)
    return jnp.dot(weights, v_rows, preferred_element_type=jnp.float32).astype(jnp.bfloat16)


def shards(seq_count, queries, keys, values, segment_ids, packing, out_weight):
    tok_rows = queries.shape[0]
    q_cols = queries.shape[1]
    kv_cols = keys.shape[1]
    shard_index = lax.axis_index(SEQ)
    per_shard = tok_rows // BLOCK
    blocks_all = packing.shape[0]

    kv_local = jnp.concatenate([keys, values], axis=1)
    kv_all = lax.all_gather(kv_local, SEQ, axis=0, tiled=True)
    kv_blocks = kv_all.reshape(blocks_all, BLOCK, 2 * kv_cols)
    target = packing[:, 0] * per_shard + packing[:, 1]
    source = jnp.zeros((blocks_all,), jnp.int32).at[target].set(
        jnp.arange(blocks_all, dtype=jnp.int32)
    )
    span_blocks = WINDOW // BLOCK
    ctx_blocks = span_blocks + per_shard
    blk_ids = shard_index * per_shard - span_blocks + jnp.arange(ctx_blocks, dtype=jnp.int32)
    src = jnp.take(source, jnp.clip(blk_ids, 0, blocks_all - 1))
    context = jnp.take(kv_blocks, src, axis=0).reshape(ctx_blocks * BLOCK, 2 * kv_cols)

    own_blocks = queries.reshape(per_shard, BLOCK, q_cols)
    own_list = lax.dynamic_slice_in_dim(packing, shard_index * per_shard, per_shard, 0)
    slot_ids = jnp.arange(seq_count, dtype=jnp.int32)
    routing = (own_list[:, 0][None, :] == slot_ids[:, None]).astype(jnp.bfloat16)
    outgoing = jnp.einsum(
        "db,brc->drc", routing, own_blocks, preferred_element_type=jnp.float32
    ).astype(jnp.bfloat16)
    incoming = lax.all_to_all(outgoing, SEQ, split_axis=0, concat_axis=0, tiled=True)
    arriving = packing[:, 0] == shard_index
    offset_ids = jnp.arange(per_shard, dtype=jnp.int32)
    at_offset = ((packing[:, 1][None, :] == offset_ids[:, None]) & arriving[None, :]).astype(
        jnp.float32
    )
    senders = jnp.arange(blocks_all, dtype=jnp.int32) // per_shard
    from_sender = (senders[:, None] == slot_ids[None, :]).astype(jnp.float32)
    placing = jnp.dot(at_offset, from_sender, precision=lax.Precision.HIGHEST).astype(jnp.bfloat16)
    packed = jnp.einsum(
        "od,drc->orc", placing, incoming, preferred_element_type=jnp.float32
    ).astype(jnp.bfloat16)
    queries_here = packed.reshape(tok_rows, q_cols)

    w_swapped = lax.ppermute(out_weight, ("ylo", "yhi"), perm=[(0, 0), (1, 2), (2, 1), (3, 3)])
    w_cols = lax.all_gather(w_swapped, "x", axis=1, tiled=True)
    w_here = lax.all_gather(w_cols, "ylo", axis=0, tiled=True)
    context, w_here = lax.optimization_barrier((context, w_here))

    ctx_keys = context[:, :kv_cols]
    ctx_values = context[:, kv_cols:]
    ctx_rows = context.shape[0]
    q_pos = shard_index * tok_rows + jnp.arange(tok_rows, dtype=jnp.int32)
    k_pos = shard_index * tok_rows - WINDOW + jnp.arange(ctx_rows, dtype=jnp.int32)
    padded_seg = jnp.concatenate([jnp.full((WINDOW,), -1, jnp.int32), segment_ids], axis=0)
    q_seg = lax.dynamic_slice_in_dim(segment_ids, shard_index * tok_rows, tok_rows, 0)
    k_seg = lax.dynamic_slice_in_dim(padded_seg, shard_index * tok_rows, ctx_rows, 0)
    heads_here = q_cols // HEAD_DIM

    def one_head(head_index):
        q_head = lax.dynamic_slice_in_dim(queries_here, head_index * HEAD_DIM, HEAD_DIM, 1)
        return attend_head(q_head, ctx_keys, ctx_values, q_pos, k_pos, q_seg, k_seg)

    per_head = lax.map(one_head, jnp.arange(heads_here, dtype=jnp.int32))
    attended = jnp.transpose(per_head, (1, 0, 2)).reshape(tok_rows, q_cols)

    h_groups = lax.all_gather(attended, "yhi", axis=1, tiled=True)
    h_here = lax.all_gather(h_groups, "c", axis=0, tiled=True)
    part = jnp.dot(h_here, w_here, preferred_element_type=jnp.float32).astype(jnp.bfloat16)
    summed = lax.psum_scatter(part, "z", scatter_dimension=1, tiled=True)
    swapped = lax.all_to_all(summed, "c", split_axis=0, concat_axis=0, tiled=True)
    return jnp.concatenate([swapped[:tok_rows], swapped[tok_rows:]], axis=1)


def solution(mesh):
    seq_count, tp_count = mesh.devices.shape
    fine = Mesh(mesh.devices.reshape(2, seq_count // 4, 2, 2, tp_count // 2), SEQ + TP)
    in_specs = (P(SEQ, TP), P(SEQ, TP), P(SEQ, TP), P(), P(), P(TP, SEQ))
    out_specs = P(SEQ, TP)
    return jax.shard_map(
        functools.partial(shards, seq_count),
        mesh=fine,
        in_specs=in_specs,
        out_specs=out_specs,
        check_vma=False,
    )
```

```python
import functools
import math

import jax
import jax.numpy as jnp
from jax import lax
from jax.sharding import Mesh, PartitionSpec as P

HEAD_DIM = 128
WINDOW = 4096
BLOCK = 128
SEQ = ("ylo", "x", "c")
TP = ("yhi", "z")


def attend_head(q_rows, k_rows, v_rows, q_pos, k_pos, q_seg, k_seg):
    scores = lax.dot_general(
        q_rows, k_rows, (((1,), (1,)), ((), ())), preferred_element_type=jnp.float32
    )
    scores = scores * (1.0 / math.sqrt(HEAD_DIM))
    allowed = (k_pos[None, :] <= q_pos[:, None]) & (k_pos[None, :] > q_pos[:, None] - WINDOW)
    allowed = allowed & (k_seg[None, :] == q_seg[:, None])
    scores = jnp.where(allowed, scores, -jnp.inf)
    top_score = jnp.max(scores, axis=1, keepdims=True)
    expo = jnp.exp(scores - top_score)
    weights = (expo / jnp.sum(expo, axis=1, keepdims=True)).astype(jnp.bfloat16)
    return jnp.dot(weights, v_rows, preferred_element_type=jnp.float32).astype(jnp.bfloat16)


def shards(seq_count, queries, keys, values, segment_ids, packing, out_weight):
    tok_rows = queries.shape[0]
    q_cols = queries.shape[1]
    kv_cols = keys.shape[1]
    shard_index = lax.axis_index(SEQ)
    per_shard = tok_rows // BLOCK
    blocks_all = packing.shape[0]

    kv_local = jnp.concatenate([keys, values], axis=1)
    kv_all = lax.all_gather(kv_local, SEQ, axis=0, tiled=True)
    kv_blocks = kv_all.reshape(blocks_all, BLOCK, 2 * kv_cols)
    target = packing[:, 0] * per_shard + packing[:, 1]
    source = jnp.zeros((blocks_all,), jnp.int32).at[target].set(
        jnp.arange(blocks_all, dtype=jnp.int32)
    )
    span_blocks = WINDOW // BLOCK
    ctx_blocks = span_blocks + per_shard
    blk_ids = shard_index * per_shard - span_blocks + jnp.arange(ctx_blocks, dtype=jnp.int32)
    src = jnp.take(source, jnp.clip(blk_ids, 0, blocks_all - 1))
    context = jnp.take(kv_blocks, src, axis=0).reshape(ctx_blocks * BLOCK, 2 * kv_cols)

    own_blocks = queries.reshape(per_shard, BLOCK, q_cols)
    own_list = lax.dynamic_slice_in_dim(packing, shard_index * per_shard, per_shard, 0)
    slot_ids = jnp.arange(seq_count, dtype=jnp.int32)
    routing = (own_list[:, 0][None, :] == slot_ids[:, None]).astype(jnp.bfloat16)
    outgoing = jnp.einsum(
        "db,brc->drc", routing, own_blocks, preferred_element_type=jnp.float32
    ).astype(jnp.bfloat16)
    incoming = lax.all_to_all(outgoing, SEQ, split_axis=0, concat_axis=0, tiled=True)
    arriving = packing[:, 0] == shard_index
    offset_ids = jnp.arange(per_shard, dtype=jnp.int32)
    at_offset = ((packing[:, 1][None, :] == offset_ids[:, None]) & arriving[None, :]).astype(
        jnp.float32
    )
    senders = jnp.arange(blocks_all, dtype=jnp.int32) // per_shard
    from_sender = (senders[:, None] == slot_ids[None, :]).astype(jnp.float32)
    placing = jnp.dot(at_offset, from_sender, precision=lax.Precision.HIGHEST).astype(jnp.bfloat16)
    packed = jnp.einsum(
        "od,drc->orc", placing, incoming, preferred_element_type=jnp.float32
    ).astype(jnp.bfloat16)
    queries_here = packed.reshape(tok_rows, q_cols)

    w_swapped = lax.ppermute(out_weight, ("ylo", "yhi"), perm=[(0, 0), (1, 2), (2, 1), (3, 3)])
    context, w_swapped = lax.optimization_barrier((context, w_swapped))
    w_stack = lax.all_gather(w_swapped, ("ylo", "x"), axis=0, tiled=False)
    w_rows, w_cols = out_weight.shape
    w_here = w_stack.reshape(2, -1, w_rows, w_cols).transpose(0, 2, 1, 3)
    w_here = w_here.reshape(2 * w_rows, -1)

    ctx_keys = context[:, :kv_cols]
    ctx_values = context[:, kv_cols:]
    ctx_rows = context.shape[0]
    q_pos = shard_index * tok_rows + jnp.arange(tok_rows, dtype=jnp.int32)
    k_pos = shard_index * tok_rows - WINDOW + jnp.arange(ctx_rows, dtype=jnp.int32)
    padded_seg = jnp.concatenate([jnp.full((WINDOW,), -1, jnp.int32), segment_ids], axis=0)
    q_seg = lax.dynamic_slice_in_dim(segment_ids, shard_index * tok_rows, tok_rows, 0)
    k_seg = lax.dynamic_slice_in_dim(padded_seg, shard_index * tok_rows, ctx_rows, 0)
    heads_here = q_cols // HEAD_DIM

    def one_head(head_index):
        q_head = lax.dynamic_slice_in_dim(queries_here, head_index * HEAD_DIM, HEAD_DIM, 1)
        return attend_head(q_head, ctx_keys, ctx_values, q_pos, k_pos, q_seg, k_seg)

    per_head = lax.map(one_head, jnp.arange(heads_here, dtype=jnp.int32))
    attended = jnp.transpose(per_head, (1, 0, 2)).reshape(tok_rows, q_cols)

    pair = [(0, 1), (1, 0)]
    h_far = lax.ppermute(attended, "yhi", pair)
    low_hi = lax.axis_index("yhi") == 0
    h_groups = jnp.where(
        low_hi,
        jnp.concatenate([attended, h_far], axis=1),
        jnp.concatenate([h_far, attended], axis=1),
    )
    h_near = lax.ppermute(h_groups, "c", pair)
    low_core = lax.axis_index("c") == 0
    h_here = jnp.where(
        low_core,
        jnp.concatenate([h_groups, h_near], axis=0),
        jnp.concatenate([h_near, h_groups], axis=0),
    )
    part = jnp.dot(h_here, w_here, preferred_element_type=jnp.float32).astype(jnp.bfloat16)
    summed = lax.psum_scatter(part, "z", scatter_dimension=1, tiled=True)
    swapped = lax.all_to_all(summed, "c", split_axis=0, concat_axis=0, tiled=True)
    return jnp.concatenate([swapped[:tok_rows], swapped[tok_rows:]], axis=1)


def solution(mesh):
    seq_count, tp_count = mesh.devices.shape
    fine = Mesh(mesh.devices.reshape(2, seq_count // 4, 2, 2, tp_count // 2), SEQ + TP)
    in_specs = (P(SEQ, TP), P(SEQ, TP), P(SEQ, TP), P(), P(), P(TP, SEQ))
    out_specs = P(SEQ, TP)
    return jax.shard_map(
        functools.partial(shards, seq_count),
        mesh=fine,
        in_specs=in_specs,
        out_specs=out_specs,
        check_vma=False,
    )
```

```python
import functools
import math

import jax
import jax.numpy as jnp
from jax import lax
from jax.sharding import Mesh, PartitionSpec as P

HEAD_DIM = 128
WINDOW = 4096
BLOCK = 128
SEQ = ("ylo", "x", "c")
TP = ("yhi", "z")


def attend_head(q_rows, k_rows, v_rows, q_pos, k_pos, q_seg, k_seg):
    scores = lax.dot_general(
        q_rows, k_rows, (((1,), (1,)), ((), ())), preferred_element_type=jnp.float32
    )
    scores = scores * (1.0 / math.sqrt(HEAD_DIM))
    allowed = (k_pos[None, :] <= q_pos[:, None]) & (k_pos[None, :] > q_pos[:, None] - WINDOW)
    allowed = allowed & (k_seg[None, :] == q_seg[:, None])
    scores = jnp.where(allowed, scores, -jnp.inf)
    top_score = jnp.max(scores, axis=1, keepdims=True)
    expo = jnp.exp(scores - top_score)
    weights = (expo / jnp.sum(expo, axis=1, keepdims=True)).astype(jnp.bfloat16)
    return jnp.dot(weights, v_rows, preferred_element_type=jnp.float32).astype(jnp.bfloat16)


def shards(seq_count, queries, keys, values, segment_ids, packing, out_weight):
    tok_rows = queries.shape[0]
    q_cols = queries.shape[1]
    kv_cols = keys.shape[1]
    shard_index = lax.axis_index(SEQ)
    per_shard = tok_rows // BLOCK
    blocks_all = packing.shape[0]

    kv_local = jnp.concatenate([keys, values], axis=1)
    kv_all = lax.all_gather(kv_local, SEQ, axis=0, tiled=True)
    kv_blocks = kv_all.reshape(blocks_all, BLOCK, 2 * kv_cols)
    target = packing[:, 0] * per_shard + packing[:, 1]
    source = jnp.zeros((blocks_all,), jnp.int32).at[target].set(
        jnp.arange(blocks_all, dtype=jnp.int32)
    )
    span_blocks = WINDOW // BLOCK
    ctx_blocks = span_blocks + per_shard
    blk_ids = shard_index * per_shard - span_blocks + jnp.arange(ctx_blocks, dtype=jnp.int32)
    src = jnp.take(source, jnp.clip(blk_ids, 0, blocks_all - 1))
    context = jnp.take(kv_blocks, src, axis=0).reshape(ctx_blocks * BLOCK, 2 * kv_cols)

    own_blocks = queries.reshape(per_shard, BLOCK, q_cols)
    own_list = lax.dynamic_slice_in_dim(packing, shard_index * per_shard, per_shard, 0)
    slot_ids = jnp.arange(seq_count, dtype=jnp.int32)
    routing = (own_list[:, 0][None, :] == slot_ids[:, None]).astype(jnp.bfloat16)
    outgoing = jnp.einsum(
        "db,brc->drc", routing, own_blocks, preferred_element_type=jnp.float32
    ).astype(jnp.bfloat16)
    incoming = lax.all_to_all(outgoing, SEQ, split_axis=0, concat_axis=0, tiled=True)
    arriving = packing[:, 0] == shard_index
    offset_ids = jnp.arange(per_shard, dtype=jnp.int32)
    at_offset = ((packing[:, 1][None, :] == offset_ids[:, None]) & arriving[None, :]).astype(
        jnp.float32
    )
    senders = jnp.arange(blocks_all, dtype=jnp.int32) // per_shard
    from_sender = (senders[:, None] == slot_ids[None, :]).astype(jnp.float32)
    placing = jnp.dot(at_offset, from_sender, precision=lax.Precision.HIGHEST).astype(jnp.bfloat16)
    packed = jnp.einsum(
        "od,drc->orc", placing, incoming, preferred_element_type=jnp.float32
    ).astype(jnp.bfloat16)
    queries_here = packed.reshape(tok_rows, q_cols)

    w_swapped = lax.ppermute(out_weight, ("ylo", "yhi"), perm=[(0, 0), (1, 2), (2, 1), (3, 3)])
    context, w_swapped = lax.optimization_barrier((context, w_swapped))
    w_here = lax.all_gather(w_swapped, ("ylo", "x"), axis=1, tiled=True)

    ctx_keys = context[:, :kv_cols]
    ctx_values = context[:, kv_cols:]
    ctx_rows = context.shape[0]
    q_pos = shard_index * tok_rows + jnp.arange(tok_rows, dtype=jnp.int32)
    k_pos = shard_index * tok_rows - WINDOW + jnp.arange(ctx_rows, dtype=jnp.int32)
    padded_seg = jnp.concatenate([jnp.full((WINDOW,), -1, jnp.int32), segment_ids], axis=0)
    q_seg = lax.dynamic_slice_in_dim(segment_ids, shard_index * tok_rows, tok_rows, 0)
    k_seg = lax.dynamic_slice_in_dim(padded_seg, shard_index * tok_rows, ctx_rows, 0)
    heads_here = q_cols // HEAD_DIM

    def one_head(head_index):
        q_head = lax.dynamic_slice_in_dim(queries_here, head_index * HEAD_DIM, HEAD_DIM, 1)
        return attend_head(q_head, ctx_keys, ctx_values, q_pos, k_pos, q_seg, k_seg)

    pair = [(0, 1), (1, 0)]
    low_hi = lax.axis_index("yhi") == 0
    low_core = lax.axis_index("c") == 0
    half = heads_here // 2
    half_cols = half * HEAD_DIM
    w_half = w_here.shape[1] // 2
    part = None
    for first in (0, half):
        per_head = lax.map(one_head, jnp.arange(first, first + half, dtype=jnp.int32))
        attended = jnp.transpose(per_head, (1, 0, 2)).reshape(tok_rows, half_cols)
        h_far = lax.ppermute(attended, "yhi", pair)
        h_groups = jnp.where(
            low_hi,
            jnp.concatenate([attended, h_far], axis=1),
            jnp.concatenate([h_far, attended], axis=1),
        )
        h_near = lax.ppermute(h_groups, "c", pair)
        h_here = jnp.where(
            low_core,
            jnp.concatenate([h_groups, h_near], axis=0),
            jnp.concatenate([h_near, h_groups], axis=0),
        )
        for group in range(2):
            rows = w_here[first * HEAD_DIM:first * HEAD_DIM + half_cols, group * w_half:(group + 1) * w_half]
            term = jnp.dot(
                h_here[:, group * half_cols:(group + 1) * half_cols],
                rows,
                preferred_element_type=jnp.float32,
            )
            part = term if part is None else part + term
    part = part.astype(jnp.bfloat16)
    summed = lax.psum_scatter(part, "z", scatter_dimension=1, tiled=True)
    swapped = lax.all_to_all(summed, "c", split_axis=0, concat_axis=0, tiled=True)
    return jnp.concatenate([swapped[:tok_rows], swapped[tok_rows:]], axis=1)


def solution(mesh):
    seq_count, tp_count = mesh.devices.shape
    fine = Mesh(mesh.devices.reshape(2, seq_count // 4, 2, 2, tp_count // 2), SEQ + TP)
    in_specs = (P(SEQ, TP), P(SEQ, TP), P(SEQ, TP), P(), P(), P(TP, SEQ))
    out_specs = P(SEQ, TP)
    return jax.shard_map(
        functools.partial(shards, seq_count),
        mesh=fine,
        in_specs=in_specs,
        out_specs=out_specs,
        check_vma=False,
    )
```

```python
import functools
import math

import jax
import jax.numpy as jnp
from jax import lax
from jax.sharding import Mesh, PartitionSpec as P

HEAD_DIM = 128
WINDOW = 4096
BLOCK = 128
SEQ = ("ylo", "x", "c")
TP = ("yhi", "z")


def attend_head(q_rows, k_rows, v_rows, q_pos, k_pos, q_seg, k_seg):
    scores = lax.dot_general(
        q_rows, k_rows, (((1,), (1,)), ((), ())), preferred_element_type=jnp.float32
    )
    scores = scores * (1.0 / math.sqrt(HEAD_DIM))
    allowed = (k_pos[None, :] <= q_pos[:, None]) & (k_pos[None, :] > q_pos[:, None] - WINDOW)
    allowed = allowed & (k_seg[None, :] == q_seg[:, None])
    scores = jnp.where(allowed, scores, -jnp.inf)
    top_score = jnp.max(scores, axis=1, keepdims=True)
    expo = jnp.exp(scores - top_score)
    weights = (expo / jnp.sum(expo, axis=1, keepdims=True)).astype(jnp.bfloat16)
    return jnp.dot(weights, v_rows, preferred_element_type=jnp.float32).astype(jnp.bfloat16)


def shards(seq_count, queries, keys, values, segment_ids, packing, out_weight):
    tok_rows = queries.shape[0]
    q_cols = queries.shape[1]
    kv_cols = keys.shape[1]
    shard_index = lax.axis_index(SEQ)
    per_shard = tok_rows // BLOCK
    blocks_all = packing.shape[0]

    kv_local = jnp.concatenate([keys, values], axis=1)
    kv_all = lax.all_gather(kv_local, SEQ, axis=0, tiled=True)
    kv_blocks = kv_all.reshape(blocks_all, BLOCK, 2 * kv_cols)
    target = packing[:, 0] * per_shard + packing[:, 1]
    source = jnp.zeros((blocks_all,), jnp.int32).at[target].set(
        jnp.arange(blocks_all, dtype=jnp.int32)
    )
    span_blocks = WINDOW // BLOCK
    ctx_blocks = span_blocks + per_shard
    blk_ids = shard_index * per_shard - span_blocks + jnp.arange(ctx_blocks, dtype=jnp.int32)
    src = jnp.take(source, jnp.clip(blk_ids, 0, blocks_all - 1))
    context = jnp.take(kv_blocks, src, axis=0).reshape(ctx_blocks * BLOCK, 2 * kv_cols)

    own_blocks = queries.reshape(per_shard, BLOCK, q_cols)
    own_list = lax.dynamic_slice_in_dim(packing, shard_index * per_shard, per_shard, 0)
    slot_ids = jnp.arange(seq_count, dtype=jnp.int32)
    routing = (own_list[:, 0][None, :] == slot_ids[:, None]).astype(jnp.bfloat16)
    outgoing = jnp.einsum(
        "db,brc->drc", routing, own_blocks, preferred_element_type=jnp.float32
    ).astype(jnp.bfloat16)
    incoming = lax.all_to_all(outgoing, SEQ, split_axis=0, concat_axis=0, tiled=True)
    arriving = packing[:, 0] == shard_index
    offset_ids = jnp.arange(per_shard, dtype=jnp.int32)
    at_offset = ((packing[:, 1][None, :] == offset_ids[:, None]) & arriving[None, :]).astype(
        jnp.float32
    )
    senders = jnp.arange(blocks_all, dtype=jnp.int32) // per_shard
    from_sender = (senders[:, None] == slot_ids[None, :]).astype(jnp.float32)
    placing = jnp.dot(at_offset, from_sender, precision=lax.Precision.HIGHEST).astype(jnp.bfloat16)
    packed = jnp.einsum(
        "od,drc->orc", placing, incoming, preferred_element_type=jnp.float32
    ).astype(jnp.bfloat16)
    queries_here = packed.reshape(tok_rows, q_cols)

    w_swapped = lax.ppermute(out_weight, ("ylo", "yhi"), perm=[(0, 0), (1, 2), (2, 1), (3, 3)])
    context, w_swapped = lax.optimization_barrier((context, w_swapped))
    w_here = lax.all_gather(w_swapped, ("x", "ylo"), axis=0, tiled=True)
    w_here = w_here.reshape(-1, 2 * out_weight.shape[0], out_weight.shape[1])

    ctx_keys = context[:, :kv_cols]
    ctx_values = context[:, kv_cols:]
    ctx_rows = context.shape[0]
    q_pos = shard_index * tok_rows + jnp.arange(tok_rows, dtype=jnp.int32)
    k_pos = shard_index * tok_rows - WINDOW + jnp.arange(ctx_rows, dtype=jnp.int32)
    padded_seg = jnp.concatenate([jnp.full((WINDOW,), -1, jnp.int32), segment_ids], axis=0)
    q_seg = lax.dynamic_slice_in_dim(segment_ids, shard_index * tok_rows, tok_rows, 0)
    k_seg = lax.dynamic_slice_in_dim(padded_seg, shard_index * tok_rows, ctx_rows, 0)
    heads_here = q_cols // HEAD_DIM

    def one_head(head_index):
        q_head = lax.dynamic_slice_in_dim(queries_here, head_index * HEAD_DIM, HEAD_DIM, 1)
        return attend_head(q_head, ctx_keys, ctx_values, q_pos, k_pos, q_seg, k_seg)

    per_head = lax.map(one_head, jnp.arange(heads_here, dtype=jnp.int32))
    attended = jnp.transpose(per_head, (1, 0, 2)).reshape(tok_rows, q_cols)

    pair = [(0, 1), (1, 0)]
    h_far = lax.ppermute(attended, "yhi", pair)
    low_hi = lax.axis_index("yhi") == 0
    h_groups = jnp.where(
        low_hi,
        jnp.concatenate([attended, h_far], axis=1),
        jnp.concatenate([h_far, attended], axis=1),
    )
    h_near = lax.ppermute(h_groups, "c", pair)
    low_core = lax.axis_index("c") == 0
    h_here = jnp.where(
        low_core,
        jnp.concatenate([h_groups, h_near], axis=0),
        jnp.concatenate([h_near, h_groups], axis=0),
    )
    part = lax.dot_general(
        h_here, w_here, (((1,), (1,)), ((), ())), preferred_element_type=jnp.float32
    )
    part = part.astype(jnp.bfloat16).reshape(h_here.shape[0], -1)
    summed = lax.psum_scatter(part, "z", scatter_dimension=1, tiled=True)
    swapped = lax.all_to_all(summed, "c", split_axis=0, concat_axis=0, tiled=True)
    return jnp.concatenate([swapped[:tok_rows], swapped[tok_rows:]], axis=1)


def solution(mesh):
    seq_count, tp_count = mesh.devices.shape
    fine = Mesh(mesh.devices.reshape(2, seq_count // 4, 2, 2, tp_count // 2), SEQ + TP)
    in_specs = (P(SEQ, TP), P(SEQ, TP), P(SEQ, TP), P(), P(), P(TP, SEQ))
    out_specs = P(SEQ, TP)
    return jax.shard_map(
        functools.partial(shards, seq_count),
        mesh=fine,
        in_specs=in_specs,
        out_specs=out_specs,
        check_vma=False,
    )
```

```python
import functools
import math

import jax
import jax.numpy as jnp
from jax import lax
from jax.sharding import Mesh, PartitionSpec as P

HEAD_DIM = 128
WINDOW = 4096
BLOCK = 128
SEQ = ("ylo", "x", "c")
TP = ("yhi", "z")


def attend_head(q_rows, k_rows, v_rows, q_pos, k_pos, q_seg, k_seg):
    scores = lax.dot_general(
        q_rows, k_rows, (((1,), (1,)), ((), ())), preferred_element_type=jnp.float32
    )
    scores = scores * (1.0 / math.sqrt(HEAD_DIM))
    allowed = (k_pos[None, :] <= q_pos[:, None]) & (k_pos[None, :] > q_pos[:, None] - WINDOW)
    allowed = allowed & (k_seg[None, :] == q_seg[:, None])
    scores = jnp.where(allowed, scores, -jnp.inf)
    top_score = jnp.max(scores, axis=1, keepdims=True)
    expo = jnp.exp(scores - top_score)
    weights = (expo / jnp.sum(expo, axis=1, keepdims=True)).astype(jnp.bfloat16)
    return jnp.dot(weights, v_rows, preferred_element_type=jnp.float32).astype(jnp.bfloat16)


def shards(seq_count, queries, keys, values, segment_ids, packing, out_weight):
    tok_rows = queries.shape[0]
    q_cols = queries.shape[1]
    kv_cols = keys.shape[1]
    shard_index = lax.axis_index(SEQ)
    per_shard = tok_rows // BLOCK
    blocks_all = packing.shape[0]

    kv_local = jnp.concatenate([keys, values], axis=1)
    kv_all = lax.all_gather(kv_local, SEQ, axis=0, tiled=True)
    kv_blocks = kv_all.reshape(blocks_all, BLOCK, 2 * kv_cols)
    target = packing[:, 0] * per_shard + packing[:, 1]
    source = jnp.zeros((blocks_all,), jnp.int32).at[target].set(
        jnp.arange(blocks_all, dtype=jnp.int32)
    )
    span_blocks = WINDOW // BLOCK
    ctx_blocks = span_blocks + per_shard
    blk_ids = shard_index * per_shard - span_blocks + jnp.arange(ctx_blocks, dtype=jnp.int32)
    src = jnp.take(source, jnp.clip(blk_ids, 0, blocks_all - 1))
    context = jnp.take(kv_blocks, src, axis=0).reshape(ctx_blocks * BLOCK, 2 * kv_cols)

    own_blocks = queries.reshape(per_shard, BLOCK, q_cols)
    own_list = lax.dynamic_slice_in_dim(packing, shard_index * per_shard, per_shard, 0)
    slot_ids = jnp.arange(seq_count, dtype=jnp.int32)
    routing = (own_list[:, 0][None, :] == slot_ids[:, None]).astype(jnp.bfloat16)
    outgoing = jnp.einsum(
        "db,brc->drc", routing, own_blocks, preferred_element_type=jnp.float32
    ).astype(jnp.bfloat16)
    incoming = lax.all_to_all(outgoing, SEQ, split_axis=0, concat_axis=0, tiled=True)
    arriving = packing[:, 0] == shard_index
    offset_ids = jnp.arange(per_shard, dtype=jnp.int32)
    at_offset = ((packing[:, 1][None, :] == offset_ids[:, None]) & arriving[None, :]).astype(
        jnp.float32
    )
    senders = jnp.arange(blocks_all, dtype=jnp.int32) // per_shard
    from_sender = (senders[:, None] == slot_ids[None, :]).astype(jnp.float32)
    placing = jnp.dot(at_offset, from_sender, precision=lax.Precision.HIGHEST).astype(jnp.bfloat16)
    packed = jnp.einsum(
        "od,drc->orc", placing, incoming, preferred_element_type=jnp.float32
    ).astype(jnp.bfloat16)
    queries_here = packed.reshape(tok_rows, q_cols)

    w_swapped = lax.ppermute(out_weight, ("ylo", "yhi"), perm=[(0, 0), (1, 2), (2, 1), (3, 3)])
    context, w_swapped = lax.optimization_barrier((context, w_swapped))
    w_here = lax.all_gather(w_swapped, ("ylo", "x"), axis=0, tiled=True)
    w_here = w_here.reshape(2, -1, out_weight.shape[0], out_weight.shape[1])

    ctx_keys = context[:, :kv_cols]
    ctx_values = context[:, kv_cols:]
    ctx_rows = context.shape[0]
    q_pos = shard_index * tok_rows + jnp.arange(tok_rows, dtype=jnp.int32)
    k_pos = shard_index * tok_rows - WINDOW + jnp.arange(ctx_rows, dtype=jnp.int32)
    padded_seg = jnp.concatenate([jnp.full((WINDOW,), -1, jnp.int32), segment_ids], axis=0)
    q_seg = lax.dynamic_slice_in_dim(segment_ids, shard_index * tok_rows, tok_rows, 0)
    k_seg = lax.dynamic_slice_in_dim(padded_seg, shard_index * tok_rows, ctx_rows, 0)
    heads_here = q_cols // HEAD_DIM

    def one_head(head_index):
        q_head = lax.dynamic_slice_in_dim(queries_here, head_index * HEAD_DIM, HEAD_DIM, 1)
        return attend_head(q_head, ctx_keys, ctx_values, q_pos, k_pos, q_seg, k_seg)

    per_head = lax.map(one_head, jnp.arange(heads_here, dtype=jnp.int32))
    attended = jnp.transpose(per_head, (1, 0, 2)).reshape(tok_rows, q_cols)

    pair = [(0, 1), (1, 0)]
    h_far = lax.ppermute(attended, "yhi", pair)
    low_hi = lax.axis_index("yhi") == 0
    h_groups = jnp.where(
        low_hi,
        jnp.concatenate([attended, h_far], axis=1),
        jnp.concatenate([h_far, attended], axis=1),
    )
    h_near = lax.ppermute(h_groups, "c", pair)
    low_core = lax.axis_index("c") == 0
    h_here = jnp.where(
        low_core,
        jnp.concatenate([h_groups, h_near], axis=0),
        jnp.concatenate([h_near, h_groups], axis=0),
    )
    h_split = h_here.reshape(h_here.shape[0], 2, -1)
    part = lax.dot_general(
        h_split, w_here, (((1, 2), (0, 2)), ((), ())), preferred_element_type=jnp.float32
    )
    part = part.astype(jnp.bfloat16).reshape(h_here.shape[0], -1)
    summed = lax.psum_scatter(part, "z", scatter_dimension=1, tiled=True)
    swapped = lax.all_to_all(summed, "c", split_axis=0, concat_axis=0, tiled=True)
    return jnp.concatenate([swapped[:tok_rows], swapped[tok_rows:]], axis=1)


def solution(mesh):
    seq_count, tp_count = mesh.devices.shape
    fine = Mesh(mesh.devices.reshape(2, seq_count // 4, 2, 2, tp_count // 2), SEQ + TP)
    in_specs = (P(SEQ, TP), P(SEQ, TP), P(SEQ, TP), P(), P(), P(TP, SEQ))
    out_specs = P(SEQ, TP)
    return jax.shard_map(
        functools.partial(shards, seq_count),
        mesh=fine,
        in_specs=in_specs,
        out_specs=out_specs,
        check_vma=False,
    )
```

```python
import functools
import math

import jax
import jax.numpy as jnp
from jax import lax
from jax.sharding import Mesh, PartitionSpec as P

HEAD_DIM = 128
WINDOW = 4096
BLOCK = 128
SEQ = ("ylo", "x", "c")
TP = ("yhi", "z")


def attend_head(q_rows, k_rows, v_rows, q_pos, k_pos, q_seg, k_seg):
    scores = lax.dot_general(
        q_rows, k_rows, (((1,), (1,)), ((), ())), preferred_element_type=jnp.float32
    )
    scores = scores * (1.0 / math.sqrt(HEAD_DIM))
    allowed = (k_pos[None, :] <= q_pos[:, None]) & (k_pos[None, :] > q_pos[:, None] - WINDOW)
    allowed = allowed & (k_seg[None, :] == q_seg[:, None])
    scores = jnp.where(allowed, scores, -jnp.inf)
    top_score = jnp.max(scores, axis=1, keepdims=True)
    expo = jnp.exp(scores - top_score)
    weights = (expo / jnp.sum(expo, axis=1, keepdims=True)).astype(jnp.bfloat16)
    return jnp.dot(weights, v_rows, preferred_element_type=jnp.float32).astype(jnp.bfloat16)


def shards(seq_count, queries, keys, values, segment_ids, packing, out_weight):
    tok_rows = queries.shape[0]
    q_cols = queries.shape[1]
    kv_cols = keys.shape[1]
    shard_index = lax.axis_index(SEQ)
    per_shard = tok_rows // BLOCK
    blocks_all = packing.shape[0]

    kv_local = jnp.concatenate([keys, values], axis=1)
    target = packing[:, 0] * per_shard + packing[:, 1]
    source = jnp.zeros((blocks_all,), jnp.int32).at[target].set(
        jnp.arange(blocks_all, dtype=jnp.int32)
    )
    span_blocks = WINDOW // BLOCK
    ctx_blocks = span_blocks + per_shard
    blk_ids = shard_index * per_shard - span_blocks + jnp.arange(ctx_blocks, dtype=jnp.int32)
    src = jnp.take(source, jnp.clip(blk_ids, 0, blocks_all - 1))

    w_swapped = lax.ppermute(out_weight, ("ylo", "yhi"), perm=[(0, 0), (1, 2), (2, 1), (3, 3)])
    kv_local, w_swapped = lax.optimization_barrier((kv_local, w_swapped))
    w_here = lax.all_gather(w_swapped, ("ylo", "x"), axis=0, tiled=True)
    w_here = w_here.reshape(2, -1, out_weight.shape[0], out_weight.shape[1])

    own_blocks = queries.reshape(per_shard, BLOCK, q_cols)
    own_list = lax.dynamic_slice_in_dim(packing, shard_index * per_shard, per_shard, 0)
    slot_ids = jnp.arange(seq_count, dtype=jnp.int32)
    routing = (own_list[:, 0][None, :] == slot_ids[:, None]).astype(jnp.bfloat16)
    outgoing = jnp.einsum(
        "db,brc->drc", routing, own_blocks, preferred_element_type=jnp.float32
    ).astype(jnp.bfloat16)
    incoming = lax.all_to_all(outgoing, SEQ, split_axis=0, concat_axis=0, tiled=True)
    kv_copies = jnp.broadcast_to(kv_local[None], (seq_count,) + kv_local.shape)
    kv_blocks = lax.all_to_all(kv_copies, SEQ, split_axis=0, concat_axis=0, tiled=True)
    kv_blocks = kv_blocks.reshape(blocks_all, BLOCK, 2 * kv_cols)
    context = jnp.take(kv_blocks, src, axis=0).reshape(ctx_blocks * BLOCK, 2 * kv_cols)
    arriving = packing[:, 0] == shard_index
    offset_ids = jnp.arange(per_shard, dtype=jnp.int32)
    at_offset = ((packing[:, 1][None, :] == offset_ids[:, None]) & arriving[None, :]).astype(
        jnp.float32
    )
    senders = jnp.arange(blocks_all, dtype=jnp.int32) // per_shard
    from_sender = (senders[:, None] == slot_ids[None, :]).astype(jnp.float32)
    placing = jnp.dot(at_offset, from_sender, precision=lax.Precision.HIGHEST).astype(jnp.bfloat16)
    packed = jnp.einsum(
        "od,drc->orc", placing, incoming, preferred_element_type=jnp.float32
    ).astype(jnp.bfloat16)
    queries_here = packed.reshape(tok_rows, q_cols)

    ctx_keys = context[:, :kv_cols]
    ctx_values = context[:, kv_cols:]
    ctx_rows = context.shape[0]
    q_pos = shard_index * tok_rows + jnp.arange(tok_rows, dtype=jnp.int32)
    k_pos = shard_index * tok_rows - WINDOW + jnp.arange(ctx_rows, dtype=jnp.int32)
    padded_seg = jnp.concatenate([jnp.full((WINDOW,), -1, jnp.int32), segment_ids], axis=0)
    q_seg = lax.dynamic_slice_in_dim(segment_ids, shard_index * tok_rows, tok_rows, 0)
    k_seg = lax.dynamic_slice_in_dim(padded_seg, shard_index * tok_rows, ctx_rows, 0)
    heads_here = q_cols // HEAD_DIM

    def one_head(head_index):
        q_head = lax.dynamic_slice_in_dim(queries_here, head_index * HEAD_DIM, HEAD_DIM, 1)
        return attend_head(q_head, ctx_keys, ctx_values, q_pos, k_pos, q_seg, k_seg)

    per_head = lax.map(one_head, jnp.arange(heads_here, dtype=jnp.int32))
    attended = jnp.transpose(per_head, (1, 0, 2)).reshape(tok_rows, q_cols)

    pair = [(0, 1), (1, 0)]
    h_far = lax.ppermute(attended, "yhi", pair)
    low_hi = lax.axis_index("yhi") == 0
    h_groups = jnp.where(
        low_hi,
        jnp.concatenate([attended, h_far], axis=1),
        jnp.concatenate([h_far, attended], axis=1),
    )
    h_near = lax.ppermute(h_groups, "c", pair)
    low_core = lax.axis_index("c") == 0
    h_here = jnp.where(
        low_core,
        jnp.concatenate([h_groups, h_near], axis=0),
        jnp.concatenate([h_near, h_groups], axis=0),
    )
    h_split = h_here.reshape(h_here.shape[0], 2, -1)
    part = lax.dot_general(
        h_split, w_here, (((1, 2), (0, 2)), ((), ())), preferred_element_type=jnp.float32
    )
    part = part.astype(jnp.bfloat16).reshape(h_here.shape[0], -1)
    summed = lax.psum_scatter(part, "z", scatter_dimension=1, tiled=True)
    swapped = lax.all_to_all(summed, "c", split_axis=0, concat_axis=0, tiled=True)
    return jnp.concatenate([swapped[:tok_rows], swapped[tok_rows:]], axis=1)


def solution(mesh):
    seq_count, tp_count = mesh.devices.shape
    fine = Mesh(mesh.devices.reshape(2, seq_count // 4, 2, 2, tp_count // 2), SEQ + TP)
    in_specs = (P(SEQ, TP), P(SEQ, TP), P(SEQ, TP), P(), P(), P(TP, SEQ))
    out_specs = P(SEQ, TP)
    return jax.shard_map(
        functools.partial(shards, seq_count),
        mesh=fine,
        in_specs=in_specs,
        out_specs=out_specs,
        check_vma=False,
    )
```

```python
import functools
import math

import jax
import jax.numpy as jnp
from jax import lax
from jax.sharding import Mesh, PartitionSpec as P

HEAD_DIM = 128
WINDOW = 4096
BLOCK = 128
SEQ = ("ylo", "x", "c")
TP = ("yhi", "z")


def attend_head(q_rows, k_rows, v_rows, q_pos, k_pos, q_seg, k_seg):
    scores = lax.dot_general(
        q_rows, k_rows, (((1,), (1,)), ((), ())), preferred_element_type=jnp.float32
    )
    scores = scores * (1.0 / math.sqrt(HEAD_DIM))
    allowed = (k_pos[None, :] <= q_pos[:, None]) & (k_pos[None, :] > q_pos[:, None] - WINDOW)
    allowed = allowed & (k_seg[None, :] == q_seg[:, None])
    scores = jnp.where(allowed, scores, -jnp.inf)
    top_score = jnp.max(scores, axis=1, keepdims=True)
    expo = jnp.exp(scores - top_score)
    weights = (expo / jnp.sum(expo, axis=1, keepdims=True)).astype(jnp.bfloat16)
    return jnp.dot(weights, v_rows, preferred_element_type=jnp.float32).astype(jnp.bfloat16)


def shards(seq_count, queries, keys, values, segment_ids, packing, out_weight):
    tok_rows = queries.shape[0]
    q_cols = queries.shape[1]
    kv_cols = keys.shape[1]
    shard_index = lax.axis_index(SEQ)
    per_shard = tok_rows // BLOCK
    blocks_all = packing.shape[0]

    kv_local = jnp.concatenate([keys, values], axis=1)
    kv_all = lax.all_gather(kv_local, SEQ, axis=0, tiled=True)
    kv_blocks = kv_all.reshape(blocks_all, BLOCK, 2 * kv_cols)
    w_swapped = lax.ppermute(out_weight, ("ylo", "yhi"), perm=[(0, 0), (1, 2), (2, 1), (3, 3)])
    kv_blocks, w_swapped = lax.optimization_barrier((kv_blocks, w_swapped))
    w_here = lax.all_gather(w_swapped, ("ylo", "x"), axis=0, tiled=True)
    w_here = w_here.reshape(2, -1, out_weight.shape[0], out_weight.shape[1])

    target = packing[:, 0] * per_shard + packing[:, 1]
    source = jnp.zeros((blocks_all,), jnp.int32).at[target].set(
        jnp.arange(blocks_all, dtype=jnp.int32)
    )
    span_blocks = WINDOW // BLOCK
    ctx_blocks = span_blocks + per_shard
    blk_ids = shard_index * per_shard - span_blocks + jnp.arange(ctx_blocks, dtype=jnp.int32)
    src = jnp.take(source, jnp.clip(blk_ids, 0, blocks_all - 1))
    context = jnp.take(kv_blocks, src, axis=0).reshape(ctx_blocks * BLOCK, 2 * kv_cols)

    own_blocks = queries.reshape(per_shard, BLOCK, q_cols)
    own_list = lax.dynamic_slice_in_dim(packing, shard_index * per_shard, per_shard, 0)
    slot_ids = jnp.arange(seq_count, dtype=jnp.int32)
    routing = (own_list[:, 0][None, :] == slot_ids[:, None]).astype(jnp.bfloat16)
    outgoing = jnp.einsum(
        "db,brc->drc", routing, own_blocks, preferred_element_type=jnp.float32
    ).astype(jnp.bfloat16)
    incoming = lax.all_to_all(outgoing, SEQ, split_axis=0, concat_axis=0, tiled=True)
    arriving = packing[:, 0] == shard_index
    offset_ids = jnp.arange(per_shard, dtype=jnp.int32)
    at_offset = ((packing[:, 1][None, :] == offset_ids[:, None]) & arriving[None, :]).astype(
        jnp.float32
    )
    senders = jnp.arange(blocks_all, dtype=jnp.int32) // per_shard
    from_sender = (senders[:, None] == slot_ids[None, :]).astype(jnp.float32)
    placing = jnp.dot(at_offset, from_sender, precision=lax.Precision.HIGHEST).astype(jnp.bfloat16)
    packed = jnp.einsum(
        "od,drc->orc", placing, incoming, preferred_element_type=jnp.float32
    ).astype(jnp.bfloat16)
    queries_here = packed.reshape(tok_rows, q_cols)

    ctx_keys = context[:, :kv_cols]
    ctx_values = context[:, kv_cols:]
    ctx_rows = context.shape[0]
    q_pos = shard_index * tok_rows + jnp.arange(tok_rows, dtype=jnp.int32)
    k_pos = shard_index * tok_rows - WINDOW + jnp.arange(ctx_rows, dtype=jnp.int32)
    padded_seg = jnp.concatenate([jnp.full((WINDOW,), -1, jnp.int32), segment_ids], axis=0)
    q_seg = lax.dynamic_slice_in_dim(segment_ids, shard_index * tok_rows, tok_rows, 0)
    k_seg = lax.dynamic_slice_in_dim(padded_seg, shard_index * tok_rows, ctx_rows, 0)
    heads_here = q_cols // HEAD_DIM

    def one_head(head_index):
        q_head = lax.dynamic_slice_in_dim(queries_here, head_index * HEAD_DIM, HEAD_DIM, 1)
        return attend_head(q_head, ctx_keys, ctx_values, q_pos, k_pos, q_seg, k_seg)

    per_head = lax.map(one_head, jnp.arange(heads_here, dtype=jnp.int32))
    attended = jnp.transpose(per_head, (1, 0, 2)).reshape(tok_rows, q_cols)

    pair = [(0, 1), (1, 0)]
    h_far = lax.ppermute(attended, "yhi", pair)
    low_hi = lax.axis_index("yhi") == 0
    h_groups = jnp.where(
        low_hi,
        jnp.concatenate([attended, h_far], axis=1),
        jnp.concatenate([h_far, attended], axis=1),
    )
    h_near = lax.ppermute(h_groups, "c", pair)
    low_core = lax.axis_index("c") == 0
    h_here = jnp.where(
        low_core,
        jnp.concatenate([h_groups, h_near], axis=0),
        jnp.concatenate([h_near, h_groups], axis=0),
    )
    h_split = h_here.reshape(h_here.shape[0], 2, -1)
    chunk = w_here.shape[-1] // 2
    pieces = []
    for first in (0, chunk):
        part = lax.dot_general(
            h_split,
            w_here[..., first:first + chunk],
            (((1, 2), (0, 2)), ((), ())),
            preferred_element_type=jnp.float32,
        )
        part = part.astype(jnp.bfloat16).reshape(h_here.shape[0], -1)
        pieces.append(lax.psum_scatter(part, "z", scatter_dimension=1, tiled=True))
    summed = jnp.concatenate(pieces, axis=1)
    swapped = lax.all_to_all(summed, "c", split_axis=0, concat_axis=0, tiled=True)
    return jnp.concatenate([swapped[:tok_rows], swapped[tok_rows:]], axis=1)


def solution(mesh):
    seq_count, tp_count = mesh.devices.shape
    fine = Mesh(mesh.devices.reshape(2, seq_count // 4, 2, 2, tp_count // 2), SEQ + TP)
    in_specs = (P(SEQ, TP), P(SEQ, TP), P(SEQ, TP), P(), P(), P(TP, SEQ))
    out_specs = P(SEQ, TP)
    return jax.shard_map(
        functools.partial(shards, seq_count),
        mesh=fine,
        in_specs=in_specs,
        out_specs=out_specs,
        check_vma=False,
    )
```

```python
import functools
import math

import jax
import jax.numpy as jnp
from jax import lax
from jax.experimental import pallas as pl
from jax.experimental.pallas import tpu as pltpu
from jax.sharding import Mesh, PartitionSpec as P

HEAD_DIM = 128
WINDOW = 4096
BLOCK = 128
SEQ = ("ylo", "x", "c")
TP = ("yhi", "z")


def route_kernel(n_x, n_c, q_out_ref, kv_ref, q_in_ref, kv_in_ref,
                 q_send, q_recv, kv_send, kv_recv, own_sem):
    n = q_out_ref.shape[0]
    me = (lax.axis_index("ylo") * n_x + lax.axis_index("x")) * n_c + lax.axis_index("c")

    def where(r):
        return {"ylo": r // (n_x * n_c), "x": (r // n_c) % n_x, "c": r % n_c}

    barrier = pltpu.get_barrier_semaphore()
    for k in range(1, n):
        r = lax.rem(me + k, n)
        pl.semaphore_signal(barrier, inc=1, device_id=where(r), device_id_type=pl.DeviceIdType.MESH)
    pl.semaphore_wait(barrier, n - 1)

    own_q = pltpu.make_async_copy(q_out_ref.at[me], q_in_ref.at[me], own_sem.at[0])
    own_kv = pltpu.make_async_copy(kv_ref, kv_in_ref.at[me], own_sem.at[1])
    own_q.start()
    own_kv.start()
    sends = []
    for k in range(1, n):
        r = lax.rem(me + k, n)
        cq = pltpu.make_async_remote_copy(
            src_ref=q_out_ref.at[r], dst_ref=q_in_ref.at[me],
            send_sem=q_send.at[k], recv_sem=q_recv.at[me],
            device_id=where(r), device_id_type=pl.DeviceIdType.MESH)
        ckv = pltpu.make_async_remote_copy(
            src_ref=kv_ref, dst_ref=kv_in_ref.at[me],
            send_sem=kv_send.at[k], recv_sem=kv_recv.at[me],
            device_id=where(r), device_id_type=pl.DeviceIdType.MESH)
        cq.start()
        ckv.start()
        sends.append((cq, ckv))
    for cq, ckv in sends:
        cq.wait_send()
        ckv.wait_send()
    for k in range(1, n):
        s = lax.rem(me + n - k, n)
        pltpu.make_async_remote_copy(
            src_ref=q_out_ref.at[s], dst_ref=q_in_ref.at[s],
            send_sem=q_send.at[k], recv_sem=q_recv.at[s],
            device_id=where(s), device_id_type=pl.DeviceIdType.MESH).wait_recv()
        pltpu.make_async_remote_copy(
            src_ref=kv_ref, dst_ref=kv_in_ref.at[s],
            send_sem=kv_send.at[k], recv_sem=kv_recv.at[s],
            device_id=where(s), device_id_type=pl.DeviceIdType.MESH).wait_recv()
    own_q.wait()
    own_kv.wait()


def route(outgoing, kv_local, n_x, n_c):
    n = outgoing.shape[0]
    any_spec = pl.BlockSpec(memory_space=pl.ANY)
    sent = n * (outgoing[0].size + kv_local.size) * 2
    return pl.pallas_call(
        functools.partial(route_kernel, n_x, n_c),
        out_shape=(
            jax.ShapeDtypeStruct(outgoing.shape, outgoing.dtype),
            jax.ShapeDtypeStruct((n,) + kv_local.shape, kv_local.dtype),
        ),
        in_specs=[any_spec, any_spec],
        out_specs=(any_spec, any_spec),
        scratch_shapes=[
            pltpu.SemaphoreType.DMA((n,)),
            pltpu.SemaphoreType.DMA((n,)),
            pltpu.SemaphoreType.DMA((n,)),
            pltpu.SemaphoreType.DMA((n,)),
            pltpu.SemaphoreType.DMA((2,)),
        ],
        compiler_params=pltpu.CompilerParams(collective_id=0, has_side_effects=True),
        cost_estimate=pl.CostEstimate(flops=0, bytes_accessed=2 * sent, transcendentals=0),
    )(outgoing, kv_local)


def attend_head(q_rows, k_rows, v_rows, q_pos, k_pos, q_seg, k_seg):
    scores = lax.dot_general(
        q_rows, k_rows, (((1,), (1,)), ((), ())), preferred_element_type=jnp.float32
    )
    scores = scores * (1.0 / math.sqrt(HEAD_DIM))
    allowed = (k_pos[None, :] <= q_pos[:, None]) & (k_pos[None, :] > q_pos[:, None] - WINDOW)
    allowed = allowed & (k_seg[None, :] == q_seg[:, None])
    scores = jnp.where(allowed, scores, -jnp.inf)
    top_score = jnp.max(scores, axis=1, keepdims=True)
    expo = jnp.exp(scores - top_score)
    weights = (expo / jnp.sum(expo, axis=1, keepdims=True)).astype(jnp.bfloat16)
    return jnp.dot(weights, v_rows, preferred_element_type=jnp.float32).astype(jnp.bfloat16)


def shards(seq_count, n_x, n_c, queries, keys, values, segment_ids, packing, out_weight):
    tok_rows = queries.shape[0]
    q_cols = queries.shape[1]
    kv_cols = keys.shape[1]
    shard_index = lax.axis_index(SEQ)
    per_shard = tok_rows // BLOCK
    blocks_all = packing.shape[0]

    kv_local = jnp.concatenate([keys, values], axis=1)
    target = packing[:, 0] * per_shard + packing[:, 1]
    source = jnp.zeros((blocks_all,), jnp.int32).at[target].set(
        jnp.arange(blocks_all, dtype=jnp.int32)
    )
    span_blocks = WINDOW // BLOCK
    ctx_blocks = span_blocks + per_shard
    blk_ids = shard_index * per_shard - span_blocks + jnp.arange(ctx_blocks, dtype=jnp.int32)
    src = jnp.take(source, jnp.clip(blk_ids, 0, blocks_all - 1))

    own_blocks = queries.reshape(per_shard, BLOCK, q_cols)
    own_list = lax.dynamic_slice_in_dim(packing, shard_index * per_shard, per_shard, 0)
    slot_ids = jnp.arange(seq_count, dtype=jnp.int32)
    routing = (own_list[:, 0][None, :] == slot_ids[:, None]).astype(jnp.bfloat16)
    outgoing = jnp.einsum(
        "db,brc->drc", routing, own_blocks, preferred_element_type=jnp.float32
    ).astype(jnp.bfloat16)
    w_swapped = lax.ppermute(out_weight, ("ylo", "yhi"), perm=[(0, 0), (1, 2), (2, 1), (3, 3)])
    outgoing, w_swapped = lax.optimization_barrier((outgoing, w_swapped))
    w_here = lax.all_gather(w_swapped, ("ylo", "x"), axis=0, tiled=True)
    w_here = w_here.reshape(2, -1, out_weight.shape[0], out_weight.shape[1])

    incoming, kv_in = route(outgoing, kv_local, n_x, n_c)
    kv_blocks = kv_in.reshape(blocks_all, BLOCK, 2 * kv_cols)
    context = jnp.take(kv_blocks, src, axis=0).reshape(ctx_blocks * BLOCK, 2 * kv_cols)
    arriving = packing[:, 0] == shard_index
    offset_ids = jnp.arange(per_shard, dtype=jnp.int32)
    at_offset = ((packing[:, 1][None, :] == offset_ids[:, None]) & arriving[None, :]).astype(
        jnp.float32
    )
    senders = jnp.arange(blocks_all, dtype=jnp.int32) // per_shard
    from_sender = (senders[:, None] == slot_ids[None, :]).astype(jnp.float32)
    placing = jnp.dot(at_offset, from_sender, precision=lax.Precision.HIGHEST).astype(jnp.bfloat16)
    packed = jnp.einsum(
        "od,drc->orc", placing, incoming, preferred_element_type=jnp.float32
    ).astype(jnp.bfloat16)
    queries_here = packed.reshape(tok_rows, q_cols)

    ctx_keys = context[:, :kv_cols]
    ctx_values = context[:, kv_cols:]
    ctx_rows = context.shape[0]
    q_pos = shard_index * tok_rows + jnp.arange(tok_rows, dtype=jnp.int32)
    k_pos = shard_index * tok_rows - WINDOW + jnp.arange(ctx_rows, dtype=jnp.int32)
    padded_seg = jnp.concatenate([jnp.full((WINDOW,), -1, jnp.int32), segment_ids], axis=0)
    q_seg = lax.dynamic_slice_in_dim(segment_ids, shard_index * tok_rows, tok_rows, 0)
    k_seg = lax.dynamic_slice_in_dim(padded_seg, shard_index * tok_rows, ctx_rows, 0)
    heads_here = q_cols // HEAD_DIM

    def one_head(head_index):
        q_head = lax.dynamic_slice_in_dim(queries_here, head_index * HEAD_DIM, HEAD_DIM, 1)
        return attend_head(q_head, ctx_keys, ctx_values, q_pos, k_pos, q_seg, k_seg)

    per_head = lax.map(one_head, jnp.arange(heads_here, dtype=jnp.int32))
    attended = jnp.transpose(per_head, (1, 0, 2)).reshape(tok_rows, q_cols)

    pair = [(0, 1), (1, 0)]
    h_far = lax.ppermute(attended, "yhi", pair)
    low_hi = lax.axis_index("yhi") == 0
    h_groups = jnp.where(
        low_hi,
        jnp.concatenate([attended, h_far], axis=1),
        jnp.concatenate([h_far, attended], axis=1),
    )
    h_near = lax.ppermute(h_groups, "c", pair)
    low_core = lax.axis_index("c") == 0
    h_here = jnp.where(
        low_core,
        jnp.concatenate([h_groups, h_near], axis=0),
        jnp.concatenate([h_near, h_groups], axis=0),
    )
    h_split = h_here.reshape(h_here.shape[0], 2, -1)
    part = lax.dot_general(
        h_split, w_here, (((1, 2), (0, 2)), ((), ())), preferred_element_type=jnp.float32
    )
    part = part.astype(jnp.bfloat16).reshape(h_here.shape[0], -1)
    summed = lax.psum_scatter(part, "z", scatter_dimension=1, tiled=True)
    swapped = lax.all_to_all(summed, "c", split_axis=0, concat_axis=0, tiled=True)
    return jnp.concatenate([swapped[:tok_rows], swapped[tok_rows:]], axis=1)


def solution(mesh):
    seq_count, tp_count = mesh.devices.shape
    fine = Mesh(mesh.devices.reshape(2, seq_count // 4, 2, 2, tp_count // 2), SEQ + TP)
    in_specs = (P(SEQ, TP), P(SEQ, TP), P(SEQ, TP), P(), P(), P(TP, SEQ))
    out_specs = P(SEQ, TP)
    return jax.shard_map(
        functools.partial(shards, seq_count, seq_count // 4, 2),
        mesh=fine,
        in_specs=in_specs,
        out_specs=out_specs,
        check_vma=False,
    )
```

```python
import functools
import math

import jax
import jax.numpy as jnp
from jax import lax
from jax.sharding import Mesh, PartitionSpec as P

HEAD_DIM = 128
WINDOW = 4096
BLOCK = 128
SEQ = ("ylo", "x", "c")
TP = ("yhi", "z")


def attend_head(q_rows, k_rows, v_rows, q_pos, k_pos, q_seg, k_seg):
    scores = lax.dot_general(
        q_rows, k_rows, (((1,), (1,)), ((), ())), preferred_element_type=jnp.float32
    )
    scores = scores * (1.0 / math.sqrt(HEAD_DIM))
    allowed = (k_pos[None, :] <= q_pos[:, None]) & (k_pos[None, :] > q_pos[:, None] - WINDOW)
    allowed = allowed & (k_seg[None, :] == q_seg[:, None])
    scores = jnp.where(allowed, scores, -jnp.inf)
    top_score = jnp.max(scores, axis=1, keepdims=True)
    expo = jnp.exp(scores - top_score)
    weights = (expo / jnp.sum(expo, axis=1, keepdims=True)).astype(jnp.bfloat16)
    return jnp.dot(weights, v_rows, preferred_element_type=jnp.float32).astype(jnp.bfloat16)


def shards(seq_count, queries, keys, values, segment_ids, packing, out_weight):
    tok_rows = queries.shape[0]
    q_cols = queries.shape[1]
    kv_cols = keys.shape[1]
    shard_index = lax.axis_index(SEQ)
    per_shard = tok_rows // BLOCK
    blocks_all = packing.shape[0]

    kv_local = jnp.concatenate([keys, values], axis=1)
    kv_mine = lax.all_gather(kv_local, ("ylo", "x"), axis=0, tiled=False)
    kv_other = lax.ppermute(kv_mine, "c", [(0, 1), (1, 0)])
    kv_all = jnp.where(
        lax.axis_index("c") == 0,
        jnp.stack([kv_mine, kv_other], axis=1),
        jnp.stack([kv_other, kv_mine], axis=1),
    )
    kv_blocks = kv_all.reshape(blocks_all, BLOCK, 2 * kv_cols)
    target = packing[:, 0] * per_shard + packing[:, 1]
    source = jnp.zeros((blocks_all,), jnp.int32).at[target].set(
        jnp.arange(blocks_all, dtype=jnp.int32)
    )
    span_blocks = WINDOW // BLOCK
    ctx_blocks = span_blocks + per_shard
    blk_ids = shard_index * per_shard - span_blocks + jnp.arange(ctx_blocks, dtype=jnp.int32)
    src = jnp.take(source, jnp.clip(blk_ids, 0, blocks_all - 1))
    context = jnp.take(kv_blocks, src, axis=0).reshape(ctx_blocks * BLOCK, 2 * kv_cols)

    own_blocks = queries.reshape(per_shard, BLOCK, q_cols)
    own_list = lax.dynamic_slice_in_dim(packing, shard_index * per_shard, per_shard, 0)
    slot_ids = jnp.arange(seq_count, dtype=jnp.int32)
    routing = (own_list[:, 0][None, :] == slot_ids[:, None]).astype(jnp.bfloat16)
    outgoing = jnp.einsum(
        "db,brc->drc", routing, own_blocks, preferred_element_type=jnp.float32
    ).astype(jnp.bfloat16)
    incoming = lax.all_to_all(outgoing, SEQ, split_axis=0, concat_axis=0, tiled=True)
    arriving = packing[:, 0] == shard_index
    offset_ids = jnp.arange(per_shard, dtype=jnp.int32)
    at_offset = ((packing[:, 1][None, :] == offset_ids[:, None]) & arriving[None, :]).astype(
        jnp.float32
    )
    senders = jnp.arange(blocks_all, dtype=jnp.int32) // per_shard
    from_sender = (senders[:, None] == slot_ids[None, :]).astype(jnp.float32)
    placing = jnp.dot(at_offset, from_sender, precision=lax.Precision.HIGHEST).astype(jnp.bfloat16)
    packed = jnp.einsum(
        "od,drc->orc", placing, incoming, preferred_element_type=jnp.float32
    ).astype(jnp.bfloat16)
    queries_here = packed.reshape(tok_rows, q_cols)

    w_swapped = lax.ppermute(out_weight, ("ylo", "yhi"), perm=[(0, 0), (1, 2), (2, 1), (3, 3)])
    context, w_swapped = lax.optimization_barrier((context, w_swapped))
    w_here = lax.all_gather(w_swapped, ("ylo", "x"), axis=0, tiled=True)
    w_here = w_here.reshape(2, -1, out_weight.shape[0], out_weight.shape[1])

    ctx_keys = context[:, :kv_cols]
    ctx_values = context[:, kv_cols:]
    ctx_rows = context.shape[0]
    q_pos = shard_index * tok_rows + jnp.arange(tok_rows, dtype=jnp.int32)
    k_pos = shard_index * tok_rows - WINDOW + jnp.arange(ctx_rows, dtype=jnp.int32)
    padded_seg = jnp.concatenate([jnp.full((WINDOW,), -1, jnp.int32), segment_ids], axis=0)
    q_seg = lax.dynamic_slice_in_dim(segment_ids, shard_index * tok_rows, tok_rows, 0)
    k_seg = lax.dynamic_slice_in_dim(padded_seg, shard_index * tok_rows, ctx_rows, 0)
    heads_here = q_cols // HEAD_DIM

    def one_head(head_index):
        q_head = lax.dynamic_slice_in_dim(queries_here, head_index * HEAD_DIM, HEAD_DIM, 1)
        return attend_head(q_head, ctx_keys, ctx_values, q_pos, k_pos, q_seg, k_seg)

    per_head = lax.map(one_head, jnp.arange(heads_here, dtype=jnp.int32))
    attended = jnp.transpose(per_head, (1, 0, 2)).reshape(tok_rows, q_cols)

    pair = [(0, 1), (1, 0)]
    h_far = lax.ppermute(attended, "yhi", pair)
    low_hi = lax.axis_index("yhi") == 0
    h_groups = jnp.where(
        low_hi,
        jnp.concatenate([attended, h_far], axis=1),
        jnp.concatenate([h_far, attended], axis=1),
    )
    h_near = lax.ppermute(h_groups, "c", pair)
    low_core = lax.axis_index("c") == 0
    h_here = jnp.where(
        low_core,
        jnp.concatenate([h_groups, h_near], axis=0),
        jnp.concatenate([h_near, h_groups], axis=0),
    )
    h_split = h_here.reshape(h_here.shape[0], 2, -1)
    part = lax.dot_general(
        h_split, w_here, (((1, 2), (0, 2)), ((), ())), preferred_element_type=jnp.float32
    )
    part = part.astype(jnp.bfloat16).reshape(h_here.shape[0], -1)
    summed = lax.psum_scatter(part, "z", scatter_dimension=1, tiled=True)
    swapped = lax.all_to_all(summed, "c", split_axis=0, concat_axis=0, tiled=True)
    return jnp.concatenate([swapped[:tok_rows], swapped[tok_rows:]], axis=1)


def solution(mesh):
    seq_count, tp_count = mesh.devices.shape
    fine = Mesh(mesh.devices.reshape(2, seq_count // 4, 2, 2, tp_count // 2), SEQ + TP)
    in_specs = (P(SEQ, TP), P(SEQ, TP), P(SEQ, TP), P(), P(), P(TP, SEQ))
    out_specs = P(SEQ, TP)
    return jax.shard_map(
        functools.partial(shards, seq_count),
        mesh=fine,
        in_specs=in_specs,
        out_specs=out_specs,
        check_vma=False,
    )
```

```python
import functools
import math

import jax
import jax.numpy as jnp
from jax import lax
from jax.sharding import Mesh, PartitionSpec as P

HEAD_DIM = 128
WINDOW = 4096
BLOCK = 128
SEQ = ("ylo", "x", "c")
TP = ("yhi", "z")


def attend_head(q_rows, k_rows, v_rows, q_pos, k_pos, q_seg, k_seg):
    scores = lax.dot_general(
        q_rows, k_rows, (((1,), (1,)), ((), ())), preferred_element_type=jnp.float32
    )
    scores = scores * (1.0 / math.sqrt(HEAD_DIM))
    allowed = (k_pos[None, :] <= q_pos[:, None]) & (k_pos[None, :] > q_pos[:, None] - WINDOW)
    allowed = allowed & (k_seg[None, :] == q_seg[:, None])
    scores = jnp.where(allowed, scores, -jnp.inf)
    top_score = jnp.max(scores, axis=1, keepdims=True)
    expo = jnp.exp(scores - top_score)
    weights = (expo / jnp.sum(expo, axis=1, keepdims=True)).astype(jnp.bfloat16)
    return jnp.dot(weights, v_rows, preferred_element_type=jnp.float32).astype(jnp.bfloat16)


def shards(seq_count, queries, keys, values, segment_ids, packing, out_weight):
    tok_rows = queries.shape[0]
    q_cols = queries.shape[1]
    kv_cols = keys.shape[1]
    shard_index = lax.axis_index(SEQ)
    per_shard = tok_rows // BLOCK
    blocks_all = packing.shape[0]

    kv_local = jnp.concatenate([keys, values], axis=1)
    w_swapped = lax.ppermute(out_weight, ("ylo", "yhi"), perm=[(0, 0), (1, 2), (2, 1), (3, 3)])
    kv_size = kv_local.size
    both = jnp.concatenate([kv_local.reshape(-1), w_swapped.reshape(-1)])
    gathered = lax.all_gather(both, ("ylo", "x"), axis=0, tiled=False)
    kv_mine = gathered[:, :kv_size].reshape((-1,) + kv_local.shape)
    w_here = gathered[:, kv_size:].reshape((2, -1) + out_weight.shape)
    kv_other = lax.ppermute(kv_mine, "c", [(0, 1), (1, 0)])
    kv_all = jnp.where(
        lax.axis_index("c") == 0,
        jnp.stack([kv_mine, kv_other], axis=1),
        jnp.stack([kv_other, kv_mine], axis=1),
    )
    kv_blocks = kv_all.reshape(blocks_all, BLOCK, 2 * kv_cols)
    target = packing[:, 0] * per_shard + packing[:, 1]
    source = jnp.zeros((blocks_all,), jnp.int32).at[target].set(
        jnp.arange(blocks_all, dtype=jnp.int32)
    )
    span_blocks = WINDOW // BLOCK
    ctx_blocks = span_blocks + per_shard
    blk_ids = shard_index * per_shard - span_blocks + jnp.arange(ctx_blocks, dtype=jnp.int32)
    src = jnp.take(source, jnp.clip(blk_ids, 0, blocks_all - 1))
    context = jnp.take(kv_blocks, src, axis=0).reshape(ctx_blocks * BLOCK, 2 * kv_cols)

    own_blocks = queries.reshape(per_shard, BLOCK, q_cols)
    own_list = lax.dynamic_slice_in_dim(packing, shard_index * per_shard, per_shard, 0)
    slot_ids = jnp.arange(seq_count, dtype=jnp.int32)
    routing = (own_list[:, 0][None, :] == slot_ids[:, None]).astype(jnp.bfloat16)
    outgoing = jnp.einsum(
        "db,brc->drc", routing, own_blocks, preferred_element_type=jnp.float32
    ).astype(jnp.bfloat16)
    incoming = lax.all_to_all(outgoing, SEQ, split_axis=0, concat_axis=0, tiled=True)
    arriving = packing[:, 0] == shard_index
    offset_ids = jnp.arange(per_shard, dtype=jnp.int32)
    at_offset = ((packing[:, 1][None, :] == offset_ids[:, None]) & arriving[None, :]).astype(
        jnp.float32
    )
    senders = jnp.arange(blocks_all, dtype=jnp.int32) // per_shard
    from_sender = (senders[:, None] == slot_ids[None, :]).astype(jnp.float32)
    placing = jnp.dot(at_offset, from_sender, precision=lax.Precision.HIGHEST).astype(jnp.bfloat16)
    packed = jnp.einsum(
        "od,drc->orc", placing, incoming, preferred_element_type=jnp.float32
    ).astype(jnp.bfloat16)
    queries_here = packed.reshape(tok_rows, q_cols)

    ctx_keys = context[:, :kv_cols]
    ctx_values = context[:, kv_cols:]
    ctx_rows = context.shape[0]
    q_pos = shard_index * tok_rows + jnp.arange(tok_rows, dtype=jnp.int32)
    k_pos = shard_index * tok_rows - WINDOW + jnp.arange(ctx_rows, dtype=jnp.int32)
    padded_seg = jnp.concatenate([jnp.full((WINDOW,), -1, jnp.int32), segment_ids], axis=0)
    q_seg = lax.dynamic_slice_in_dim(segment_ids, shard_index * tok_rows, tok_rows, 0)
    k_seg = lax.dynamic_slice_in_dim(padded_seg, shard_index * tok_rows, ctx_rows, 0)
    heads_here = q_cols // HEAD_DIM

    def one_head(head_index):
        q_head = lax.dynamic_slice_in_dim(queries_here, head_index * HEAD_DIM, HEAD_DIM, 1)
        return attend_head(q_head, ctx_keys, ctx_values, q_pos, k_pos, q_seg, k_seg)

    per_head = lax.map(one_head, jnp.arange(heads_here, dtype=jnp.int32))
    attended = jnp.transpose(per_head, (1, 0, 2)).reshape(tok_rows, q_cols)

    pair = [(0, 1), (1, 0)]
    h_far = lax.ppermute(attended, "yhi", pair)
    low_hi = lax.axis_index("yhi") == 0
    h_groups = jnp.where(
        low_hi,
        jnp.concatenate([attended, h_far], axis=1),
        jnp.concatenate([h_far, attended], axis=1),
    )
    h_near = lax.ppermute(h_groups, "c", pair)
    low_core = lax.axis_index("c") == 0
    h_here = jnp.where(
        low_core,
        jnp.concatenate([h_groups, h_near], axis=0),
        jnp.concatenate([h_near, h_groups], axis=0),
    )
    h_split = h_here.reshape(h_here.shape[0], 2, -1)
    part = lax.dot_general(
        h_split, w_here, (((1, 2), (0, 2)), ((), ())), preferred_element_type=jnp.float32
    )
    part = part.astype(jnp.bfloat16).reshape(h_here.shape[0], -1)
    summed = lax.psum_scatter(part, "z", scatter_dimension=1, tiled=True)
    swapped = lax.all_to_all(summed, "c", split_axis=0, concat_axis=0, tiled=True)
    return jnp.concatenate([swapped[:tok_rows], swapped[tok_rows:]], axis=1)


def solution(mesh):
    seq_count, tp_count = mesh.devices.shape
    fine = Mesh(mesh.devices.reshape(2, seq_count // 4, 2, 2, tp_count // 2), SEQ + TP)
    in_specs = (P(SEQ, TP), P(SEQ, TP), P(SEQ, TP), P(), P(), P(TP, SEQ))
    out_specs = P(SEQ, TP)
    return jax.shard_map(
        functools.partial(shards, seq_count),
        mesh=fine,
        in_specs=in_specs,
        out_specs=out_specs,
        check_vma=False,
    )
```

```python
import functools
import math

import jax
import jax.numpy as jnp
from jax import lax
from jax.sharding import Mesh, PartitionSpec as P

HEAD_DIM = 128
WINDOW = 4096
BLOCK = 128
SEQ = ("ylo", "x", "c")
TP = ("yhi", "z")


def attend_head(q_rows, k_rows, v_rows, q_pos, k_pos, q_seg, k_seg):
    scores = lax.dot_general(
        q_rows, k_rows, (((1,), (1,)), ((), ())), preferred_element_type=jnp.float32
    )
    scores = scores * (1.0 / math.sqrt(HEAD_DIM))
    allowed = (k_pos[None, :] <= q_pos[:, None]) & (k_pos[None, :] > q_pos[:, None] - WINDOW)
    allowed = allowed & (k_seg[None, :] == q_seg[:, None])
    scores = jnp.where(allowed, scores, -jnp.inf)
    top_score = jnp.max(scores, axis=1, keepdims=True)
    expo = jnp.exp(scores - top_score)
    weights = (expo / jnp.sum(expo, axis=1, keepdims=True)).astype(jnp.bfloat16)
    return jnp.dot(weights, v_rows, preferred_element_type=jnp.float32).astype(jnp.bfloat16)


def shards(seq_count, queries, keys, values, segment_ids, packing, out_weight):
    tok_rows = queries.shape[0]
    q_cols = queries.shape[1]
    kv_cols = keys.shape[1]
    shard_index = lax.axis_index(SEQ)
    per_shard = tok_rows // BLOCK
    blocks_all = packing.shape[0]

    kv_local = jnp.concatenate([keys, values], axis=1)
    target = packing[:, 0] * per_shard + packing[:, 1]
    source = jnp.zeros((blocks_all,), jnp.int32).at[target].set(
        jnp.arange(blocks_all, dtype=jnp.int32)
    )
    span_blocks = WINDOW // BLOCK
    ctx_blocks = span_blocks + per_shard
    blk_ids = shard_index * per_shard - span_blocks + jnp.arange(ctx_blocks, dtype=jnp.int32)
    src = jnp.take(source, jnp.clip(blk_ids, 0, blocks_all - 1))

    own_blocks = queries.reshape(per_shard, BLOCK, q_cols)
    own_list = lax.dynamic_slice_in_dim(packing, shard_index * per_shard, per_shard, 0)
    slot_ids = jnp.arange(seq_count, dtype=jnp.int32)
    routing = (own_list[:, 0][None, :] == slot_ids[:, None]).astype(jnp.bfloat16)
    outgoing = jnp.einsum(
        "db,brc->drc", routing, own_blocks, preferred_element_type=jnp.float32
    ).astype(jnp.bfloat16)
    lanes = kv_local.shape[1]
    q_rows = BLOCK * q_cols // lanes
    payload = jnp.concatenate(
        [
            outgoing.reshape(seq_count, q_rows, lanes),
            jnp.broadcast_to(kv_local[None], (seq_count,) + kv_local.shape),
        ],
        axis=1,
    )
    arrived = lax.all_to_all(payload, SEQ, split_axis=0, concat_axis=0, tiled=True)
    incoming = arrived[:, :q_rows].reshape(seq_count, BLOCK, q_cols)
    kv_blocks = arrived[:, q_rows:].reshape(blocks_all, BLOCK, 2 * kv_cols)
    context = jnp.take(kv_blocks, src, axis=0).reshape(ctx_blocks * BLOCK, 2 * kv_cols)
    arriving = packing[:, 0] == shard_index
    offset_ids = jnp.arange(per_shard, dtype=jnp.int32)
    at_offset = ((packing[:, 1][None, :] == offset_ids[:, None]) & arriving[None, :]).astype(
        jnp.float32
    )
    senders = jnp.arange(blocks_all, dtype=jnp.int32) // per_shard
    from_sender = (senders[:, None] == slot_ids[None, :]).astype(jnp.float32)
    placing = jnp.dot(at_offset, from_sender, precision=lax.Precision.HIGHEST).astype(jnp.bfloat16)
    packed = jnp.einsum(
        "od,drc->orc", placing, incoming, preferred_element_type=jnp.float32
    ).astype(jnp.bfloat16)
    queries_here = packed.reshape(tok_rows, q_cols)

    w_swapped = lax.ppermute(out_weight, ("ylo", "yhi"), perm=[(0, 0), (1, 2), (2, 1), (3, 3)])
    w_here = lax.all_gather(w_swapped, ("ylo", "x"), axis=0, tiled=True)
    w_here = w_here.reshape(2, -1, out_weight.shape[0], out_weight.shape[1])
    context, w_here = lax.optimization_barrier((context, w_here))

    ctx_keys = context[:, :kv_cols]
    ctx_values = context[:, kv_cols:]
    ctx_rows = context.shape[0]
    q_pos = shard_index * tok_rows + jnp.arange(tok_rows, dtype=jnp.int32)
    k_pos = shard_index * tok_rows - WINDOW + jnp.arange(ctx_rows, dtype=jnp.int32)
    padded_seg = jnp.concatenate([jnp.full((WINDOW,), -1, jnp.int32), segment_ids], axis=0)
    q_seg = lax.dynamic_slice_in_dim(segment_ids, shard_index * tok_rows, tok_rows, 0)
    k_seg = lax.dynamic_slice_in_dim(padded_seg, shard_index * tok_rows, ctx_rows, 0)
    heads_here = q_cols // HEAD_DIM

    def one_head(head_index):
        q_head = lax.dynamic_slice_in_dim(queries_here, head_index * HEAD_DIM, HEAD_DIM, 1)
        return attend_head(q_head, ctx_keys, ctx_values, q_pos, k_pos, q_seg, k_seg)

    per_head = lax.map(one_head, jnp.arange(heads_here, dtype=jnp.int32))
    attended = jnp.transpose(per_head, (1, 0, 2)).reshape(tok_rows, q_cols)

    pair = [(0, 1), (1, 0)]
    h_far = lax.ppermute(attended, "yhi", pair)
    low_hi = lax.axis_index("yhi") == 0
    h_groups = jnp.where(
        low_hi,
        jnp.concatenate([attended, h_far], axis=1),
        jnp.concatenate([h_far, attended], axis=1),
    )
    h_near = lax.ppermute(h_groups, "c", pair)
    low_core = lax.axis_index("c") == 0
    h_here = jnp.where(
        low_core,
        jnp.concatenate([h_groups, h_near], axis=0),
        jnp.concatenate([h_near, h_groups], axis=0),
    )
    h_split = h_here.reshape(h_here.shape[0], 2, -1)
    part = lax.dot_general(
        h_split, w_here, (((1, 2), (0, 2)), ((), ())), preferred_element_type=jnp.float32
    )
    part = part.astype(jnp.bfloat16).reshape(h_here.shape[0], -1)
    summed = lax.psum_scatter(part, "z", scatter_dimension=1, tiled=True)
    swapped = lax.all_to_all(summed, "c", split_axis=0, concat_axis=0, tiled=True)
    return jnp.concatenate([swapped[:tok_rows], swapped[tok_rows:]], axis=1)


def solution(mesh):
    seq_count, tp_count = mesh.devices.shape
    fine = Mesh(mesh.devices.reshape(2, seq_count // 4, 2, 2, tp_count // 2), SEQ + TP)
    in_specs = (P(SEQ, TP), P(SEQ, TP), P(SEQ, TP), P(), P(), P(TP, SEQ))
    out_specs = P(SEQ, TP)
    return jax.shard_map(
        functools.partial(shards, seq_count),
        mesh=fine,
        in_specs=in_specs,
        out_specs=out_specs,
        check_vma=False,
    )
```

```python
import functools
import math

import jax
import jax.numpy as jnp
from jax import lax
from jax.sharding import Mesh, PartitionSpec as P

HEAD_DIM = 128
WINDOW = 4096
BLOCK = 128
SEQ = ("ylo", "x", "c")
TP = ("yhi", "z")


def attend_head(q_rows, k_rows, v_rows, q_pos, k_pos, q_seg, k_seg):
    scores = lax.dot_general(
        q_rows, k_rows, (((1,), (1,)), ((), ())), preferred_element_type=jnp.float32
    )
    scores = scores * (1.0 / math.sqrt(HEAD_DIM))
    allowed = (k_pos[None, :] <= q_pos[:, None]) & (k_pos[None, :] > q_pos[:, None] - WINDOW)
    allowed = allowed & (k_seg[None, :] == q_seg[:, None])
    scores = jnp.where(allowed, scores, -jnp.inf)
    top_score = jnp.max(scores, axis=1, keepdims=True)
    expo = jnp.exp(scores - top_score)
    weights = (expo / jnp.sum(expo, axis=1, keepdims=True)).astype(jnp.bfloat16)
    return jnp.dot(weights, v_rows, preferred_element_type=jnp.float32).astype(jnp.bfloat16)


def shards(seq_count, queries, keys, values, segment_ids, packing, out_weight):
    tok_rows = queries.shape[0]
    q_cols = queries.shape[1]
    kv_cols = keys.shape[1]
    shard_index = lax.axis_index(SEQ)
    per_shard = tok_rows // BLOCK
    blocks_all = packing.shape[0]

    kv_local = jnp.concatenate([keys, values], axis=1)
    kv_all = lax.all_gather(kv_local, SEQ, axis=0, tiled=True)
    kv_blocks = kv_all.reshape(blocks_all, BLOCK, 2 * kv_cols)
    w_swapped = lax.ppermute(out_weight, ("ylo", "yhi"), perm=[(0, 0), (1, 2), (2, 1), (3, 3)])
    kv_blocks, w_swapped = lax.optimization_barrier((kv_blocks, w_swapped))
    w_here = lax.all_gather(w_swapped, ("ylo", "x"), axis=0, tiled=True)
    w_here = w_here.reshape(2, -1, out_weight.shape[0], out_weight.shape[1])

    target = packing[:, 0] * per_shard + packing[:, 1]
    source = jnp.zeros((blocks_all,), jnp.int32).at[target].set(
        jnp.arange(blocks_all, dtype=jnp.int32)
    )
    span_blocks = WINDOW // BLOCK
    ctx_blocks = span_blocks + per_shard
    blk_ids = shard_index * per_shard - span_blocks + jnp.arange(ctx_blocks, dtype=jnp.int32)
    src = jnp.take(source, jnp.clip(blk_ids, 0, blocks_all - 1))
    context = jnp.take(kv_blocks, src, axis=0).reshape(ctx_blocks * BLOCK, 2 * kv_cols)

    own_blocks = queries.reshape(per_shard, BLOCK, q_cols)
    own_list = lax.dynamic_slice_in_dim(packing, shard_index * per_shard, per_shard, 0)
    slot_ids = jnp.arange(seq_count, dtype=jnp.int32)
    routing = (own_list[:, 0][None, :] == slot_ids[:, None]).astype(jnp.bfloat16)
    outgoing = jnp.einsum(
        "db,brc->drc", routing, own_blocks, preferred_element_type=jnp.float32
    ).astype(jnp.bfloat16)
    incoming = lax.all_to_all(outgoing, SEQ, split_axis=0, concat_axis=0, tiled=True)
    arriving = packing[:, 0] == shard_index
    offset_ids = jnp.arange(per_shard, dtype=jnp.int32)
    at_offset = ((packing[:, 1][None, :] == offset_ids[:, None]) & arriving[None, :]).astype(
        jnp.float32
    )
    senders = jnp.arange(blocks_all, dtype=jnp.int32) // per_shard
    from_sender = (senders[:, None] == slot_ids[None, :]).astype(jnp.float32)
    placing = jnp.dot(at_offset, from_sender, precision=lax.Precision.HIGHEST).astype(jnp.bfloat16)
    packed = jnp.einsum(
        "od,drc->orc", placing, incoming, preferred_element_type=jnp.float32
    ).astype(jnp.bfloat16)
    queries_here = packed.reshape(tok_rows, q_cols)

    ctx_keys = context[:, :kv_cols]
    ctx_values = context[:, kv_cols:]
    ctx_rows = context.shape[0]
    q_pos = shard_index * tok_rows + jnp.arange(tok_rows, dtype=jnp.int32)
    k_pos = shard_index * tok_rows - WINDOW + jnp.arange(ctx_rows, dtype=jnp.int32)
    padded_seg = jnp.concatenate([jnp.full((WINDOW,), -1, jnp.int32), segment_ids], axis=0)
    q_seg = lax.dynamic_slice_in_dim(segment_ids, shard_index * tok_rows, tok_rows, 0)
    k_seg = lax.dynamic_slice_in_dim(padded_seg, shard_index * tok_rows, ctx_rows, 0)
    heads_here = q_cols // HEAD_DIM

    def one_head(head_index):
        q_head = lax.dynamic_slice_in_dim(queries_here, head_index * HEAD_DIM, HEAD_DIM, 1)
        return attend_head(q_head, ctx_keys, ctx_values, q_pos, k_pos, q_seg, k_seg)

    per_head = lax.map(one_head, jnp.arange(heads_here, dtype=jnp.int32))
    attended = jnp.transpose(per_head, (1, 0, 2)).reshape(tok_rows, q_cols)

    pair = [(0, 1), (1, 0)]
    h_far = lax.ppermute(attended, "yhi", pair)
    low_hi = lax.axis_index("yhi") == 0
    h_groups = jnp.where(
        low_hi,
        jnp.concatenate([attended, h_far], axis=1),
        jnp.concatenate([h_far, attended], axis=1),
    )
    h_near = lax.ppermute(h_groups, "c", pair)
    low_core = lax.axis_index("c") == 0
    h_here = jnp.where(
        low_core,
        jnp.concatenate([h_groups, h_near], axis=0),
        jnp.concatenate([h_near, h_groups], axis=0),
    )
    h_split = h_here.reshape(h_here.shape[0], 2, -1)
    part = lax.dot_general(
        h_split, w_here, (((1, 2), (0, 2)), ((), ())), preferred_element_type=jnp.float32
    )
    part = part.astype(jnp.bfloat16).reshape(h_here.shape[0], -1)
    summed = lax.psum_scatter(part, "z", scatter_dimension=1, tiled=True)
    swapped = lax.all_to_all(summed, "c", split_axis=0, concat_axis=0, tiled=True)
    return jnp.concatenate([swapped[:tok_rows], swapped[tok_rows:]], axis=1)


def solution(mesh):
    seq_count, tp_count = mesh.devices.shape
    fine = Mesh(mesh.devices.reshape(2, seq_count // 4, 2, 2, tp_count // 2), SEQ + TP)
    in_specs = (P(SEQ, TP), P(SEQ, TP), P(SEQ, TP), P(), P(), P(TP, SEQ))
    out_specs = P(SEQ, TP)
    return jax.shard_map(
        functools.partial(shards, seq_count),
        mesh=fine,
        in_specs=in_specs,
        out_specs=out_specs,
        check_vma=False,
    )
```

```python
import functools
import math

import jax
import jax.numpy as jnp
from jax import lax
from jax.sharding import Mesh, PartitionSpec as P

HEAD_DIM = 128
WINDOW = 4096
BLOCK = 128
SEQ = ("ylo", "x", "c")
TP = ("yhi", "z")


def attend_head(q_rows, k_rows, v_rows, q_pos, k_pos, q_seg, k_seg):
    scores = lax.dot_general(
        q_rows, k_rows, (((1,), (1,)), ((), ())), preferred_element_type=jnp.float32
    )
    scores = scores * (1.0 / math.sqrt(HEAD_DIM))
    allowed = (k_pos[None, :] <= q_pos[:, None]) & (k_pos[None, :] > q_pos[:, None] - WINDOW)
    allowed = allowed & (k_seg[None, :] == q_seg[:, None])
    scores = jnp.where(allowed, scores, -jnp.inf)
    top_score = jnp.max(scores, axis=1, keepdims=True)
    expo = jnp.exp(scores - top_score)
    weights = (expo / jnp.sum(expo, axis=1, keepdims=True)).astype(jnp.bfloat16)
    return jnp.dot(weights, v_rows, preferred_element_type=jnp.float32).astype(jnp.bfloat16)


def shards(seq_count, queries, keys, values, segment_ids, packing, out_weight):
    tok_rows = queries.shape[0]
    q_cols = queries.shape[1]
    kv_cols = keys.shape[1]
    shard_index = lax.axis_index(SEQ)
    per_shard = tok_rows // BLOCK
    blocks_all = packing.shape[0]

    kv_local = jnp.concatenate([keys, values], axis=1)
    kv_all = lax.all_gather(kv_local, SEQ, axis=0, tiled=True)
    kv_blocks = kv_all.reshape(blocks_all, BLOCK, 2 * kv_cols)
    w_swapped = lax.ppermute(out_weight, ("ylo", "yhi"), perm=[(0, 0), (1, 2), (2, 1), (3, 3)])
    kv_blocks, w_swapped = lax.optimization_barrier((kv_blocks, w_swapped))
    w_here = lax.all_gather(w_swapped, ("ylo", "x"), axis=0, tiled=True)
    w_here = w_here.reshape(2, -1, out_weight.shape[0], out_weight.shape[1])

    target = packing[:, 0] * per_shard + packing[:, 1]
    source = jnp.zeros((blocks_all,), jnp.int32).at[target].set(
        jnp.arange(blocks_all, dtype=jnp.int32)
    )
    span_blocks = WINDOW // BLOCK
    ctx_blocks = span_blocks + per_shard
    blk_ids = shard_index * per_shard - span_blocks + jnp.arange(ctx_blocks, dtype=jnp.int32)
    src = jnp.take(source, jnp.clip(blk_ids, 0, blocks_all - 1))
    context = jnp.take(kv_blocks, src, axis=0).reshape(ctx_blocks * BLOCK, 2 * kv_cols)

    own_blocks = queries.reshape(per_shard, BLOCK, q_cols)
    own_list = lax.dynamic_slice_in_dim(packing, shard_index * per_shard, per_shard, 0)
    slot_ids = jnp.arange(seq_count, dtype=jnp.int32)
    routing = (own_list[:, 0][None, :] == slot_ids[:, None]).astype(jnp.bfloat16)
    outgoing = jnp.einsum(
        "db,brc->drc", routing, own_blocks, preferred_element_type=jnp.float32
    ).astype(jnp.bfloat16)
    incoming = lax.all_to_all(outgoing, SEQ, split_axis=0, concat_axis=0, tiled=True)
    arriving = packing[:, 0] == shard_index
    offset_ids = jnp.arange(per_shard, dtype=jnp.int32)
    at_offset = ((packing[:, 1][None, :] == offset_ids[:, None]) & arriving[None, :]).astype(
        jnp.float32
    )
    senders = jnp.arange(blocks_all, dtype=jnp.int32) // per_shard
    from_sender = (senders[:, None] == slot_ids[None, :]).astype(jnp.float32)
    placing = jnp.dot(at_offset, from_sender, precision=lax.Precision.HIGHEST).astype(jnp.bfloat16)
    packed = jnp.einsum(
        "od,drc->orc", placing, incoming, preferred_element_type=jnp.float32
    ).astype(jnp.bfloat16)
    queries_here = packed.reshape(tok_rows, q_cols)

    ctx_keys = context[:, :kv_cols]
    ctx_values = context[:, kv_cols:]
    ctx_rows = context.shape[0]
    q_pos = shard_index * tok_rows + jnp.arange(tok_rows, dtype=jnp.int32)
    k_pos = shard_index * tok_rows - WINDOW + jnp.arange(ctx_rows, dtype=jnp.int32)
    padded_seg = jnp.concatenate([jnp.full((WINDOW,), -1, jnp.int32), segment_ids], axis=0)
    q_seg = lax.dynamic_slice_in_dim(segment_ids, shard_index * tok_rows, tok_rows, 0)
    k_seg = lax.dynamic_slice_in_dim(padded_seg, shard_index * tok_rows, ctx_rows, 0)
    heads_here = q_cols // HEAD_DIM

    def one_head(head_index):
        q_head = lax.dynamic_slice_in_dim(queries_here, head_index * HEAD_DIM, HEAD_DIM, 1)
        return attend_head(q_head, ctx_keys, ctx_values, q_pos, k_pos, q_seg, k_seg)

    half = heads_here // 2
    pair = [(0, 1), (1, 0)]
    mine, far = [], []
    for first in (0, half):
        per_head = lax.map(one_head, jnp.arange(first, first + half, dtype=jnp.int32))
        piece = jnp.transpose(per_head, (1, 0, 2)).reshape(tok_rows, half * HEAD_DIM)
        mine.append(piece)
        far.append(lax.ppermute(piece, "yhi", pair))
    attended = jnp.concatenate(mine, axis=1)
    h_far = jnp.concatenate(far, axis=1)
    low_hi = lax.axis_index("yhi") == 0
    h_groups = jnp.where(
        low_hi,
        jnp.concatenate([attended, h_far], axis=1),
        jnp.concatenate([h_far, attended], axis=1),
    )
    h_near = lax.ppermute(h_groups, "c", pair)
    low_core = lax.axis_index("c") == 0
    h_here = jnp.where(
        low_core,
        jnp.concatenate([h_groups, h_near], axis=0),
        jnp.concatenate([h_near, h_groups], axis=0),
    )
    h_split = h_here.reshape(h_here.shape[0], 2, -1)
    part = lax.dot_general(
        h_split, w_here, (((1, 2), (0, 2)), ((), ())), preferred_element_type=jnp.float32
    )
    part = part.astype(jnp.bfloat16).reshape(h_here.shape[0], -1)
    summed = lax.psum_scatter(part, "z", scatter_dimension=1, tiled=True)
    swapped = lax.all_to_all(summed, "c", split_axis=0, concat_axis=0, tiled=True)
    return jnp.concatenate([swapped[:tok_rows], swapped[tok_rows:]], axis=1)


def solution(mesh):
    seq_count, tp_count = mesh.devices.shape
    fine = Mesh(mesh.devices.reshape(2, seq_count // 4, 2, 2, tp_count // 2), SEQ + TP)
    in_specs = (P(SEQ, TP), P(SEQ, TP), P(SEQ, TP), P(), P(), P(TP, SEQ))
    out_specs = P(SEQ, TP)
    return jax.shard_map(
        functools.partial(shards, seq_count),
        mesh=fine,
        in_specs=in_specs,
        out_specs=out_specs,
        check_vma=False,
    )
```

```python
import functools
import math

import jax
import jax.numpy as jnp
from jax import lax
from jax.sharding import Mesh, PartitionSpec as P

HEAD_DIM = 128
WINDOW = 4096
BLOCK = 128
SEQ = ("ylo", "x", "c")
TP = ("yhi", "z")


def attend_head(q_rows, k_rows, v_rows, q_pos, k_pos, q_seg, k_seg):
    scores = lax.dot_general(
        q_rows, k_rows, (((1,), (1,)), ((), ())), preferred_element_type=jnp.float32
    )
    scores = scores * (1.0 / math.sqrt(HEAD_DIM))
    allowed = (k_pos[None, :] <= q_pos[:, None]) & (k_pos[None, :] > q_pos[:, None] - WINDOW)
    allowed = allowed & (k_seg[None, :] == q_seg[:, None])
    scores = jnp.where(allowed, scores, -jnp.inf)
    top_score = jnp.max(scores, axis=1, keepdims=True)
    expo = jnp.exp(scores - top_score)
    weights = (expo / jnp.sum(expo, axis=1, keepdims=True)).astype(jnp.bfloat16)
    return jnp.dot(weights, v_rows, preferred_element_type=jnp.float32).astype(jnp.bfloat16)


def shards(seq_count, queries, keys, values, segment_ids, packing, out_weight):
    tok_rows = queries.shape[0]
    q_cols = queries.shape[1]
    kv_cols = keys.shape[1]
    shard_index = lax.axis_index(SEQ)
    per_shard = tok_rows // BLOCK
    blocks_all = packing.shape[0]

    kv_local = jnp.concatenate([keys, values], axis=1)
    kv_all = lax.all_gather(kv_local, SEQ, axis=0, tiled=True)
    kv_blocks = kv_all.reshape(blocks_all, BLOCK, 2 * kv_cols)
    w_swapped = lax.ppermute(out_weight, ("ylo", "yhi"), perm=[(0, 0), (1, 2), (2, 1), (3, 3)])
    kv_blocks, w_swapped = lax.optimization_barrier((kv_blocks, w_swapped))
    w_here = lax.all_gather(w_swapped, ("ylo", "x"), axis=0, tiled=True)
    w_here = w_here.reshape(2, -1, out_weight.shape[0], out_weight.shape[1])

    target = packing[:, 0] * per_shard + packing[:, 1]
    source = jnp.zeros((blocks_all,), jnp.int32).at[target].set(
        jnp.arange(blocks_all, dtype=jnp.int32)
    )
    span_blocks = WINDOW // BLOCK
    ctx_blocks = span_blocks + per_shard
    blk_ids = shard_index * per_shard - span_blocks + jnp.arange(ctx_blocks, dtype=jnp.int32)
    src = jnp.take(source, jnp.clip(blk_ids, 0, blocks_all - 1))
    context = jnp.take(kv_blocks, src, axis=0).reshape(ctx_blocks * BLOCK, 2 * kv_cols)

    own_blocks = queries.reshape(per_shard, BLOCK, q_cols)
    own_list = lax.dynamic_slice_in_dim(packing, shard_index * per_shard, per_shard, 0)
    slot_ids = jnp.arange(seq_count, dtype=jnp.int32)
    routing = (own_list[:, 0][None, :] == slot_ids[:, None]).astype(jnp.bfloat16)
    outgoing = jnp.einsum(
        "db,brc->drc", routing, own_blocks, preferred_element_type=jnp.float32
    ).astype(jnp.bfloat16)
    incoming = lax.all_to_all(outgoing, SEQ, split_axis=0, concat_axis=0, tiled=True)
    arriving = packing[:, 0] == shard_index
    offset_ids = jnp.arange(per_shard, dtype=jnp.int32)
    at_offset = ((packing[:, 1][None, :] == offset_ids[:, None]) & arriving[None, :]).astype(
        jnp.float32
    )
    senders = jnp.arange(blocks_all, dtype=jnp.int32) // per_shard
    from_sender = (senders[:, None] == slot_ids[None, :]).astype(jnp.float32)
    placing = jnp.dot(at_offset, from_sender, precision=lax.Precision.HIGHEST).astype(jnp.bfloat16)
    packed = jnp.einsum(
        "od,drc->orc", placing, incoming, preferred_element_type=jnp.float32
    ).astype(jnp.bfloat16)
    queries_here = packed.reshape(tok_rows, q_cols)

    ctx_keys = context[:, :kv_cols]
    ctx_values = context[:, kv_cols:]
    ctx_rows = context.shape[0]
    q_pos = shard_index * tok_rows + jnp.arange(tok_rows, dtype=jnp.int32)
    k_pos = shard_index * tok_rows - WINDOW + jnp.arange(ctx_rows, dtype=jnp.int32)
    padded_seg = jnp.concatenate([jnp.full((WINDOW,), -1, jnp.int32), segment_ids], axis=0)
    q_seg = lax.dynamic_slice_in_dim(segment_ids, shard_index * tok_rows, tok_rows, 0)
    k_seg = lax.dynamic_slice_in_dim(padded_seg, shard_index * tok_rows, ctx_rows, 0)
    heads_here = q_cols // HEAD_DIM

    def one_head(head_index):
        q_head = lax.dynamic_slice_in_dim(queries_here, head_index * HEAD_DIM, HEAD_DIM, 1)
        return attend_head(q_head, ctx_keys, ctx_values, q_pos, k_pos, q_seg, k_seg)

    half = heads_here // 2
    pair = [(0, 1), (1, 0)]
    mine, far = [], []
    for first in (0, half):
        per_head = lax.map(one_head, jnp.arange(first, first + half, dtype=jnp.int32))
        piece = jnp.transpose(per_head, (1, 0, 2)).reshape(tok_rows, half * HEAD_DIM)
        mine.append(piece)
        far.append(lax.ppermute(piece, "yhi", pair))
    attended = jnp.concatenate(mine, axis=1)
    low_core = lax.axis_index("c") == 0

    def both_cores(here, there):
        return jnp.where(
            low_core,
            jnp.concatenate([here, there], axis=0),
            jnp.concatenate([there, here], axis=0),
        )

    h_own = both_cores(attended, lax.ppermute(attended, "c", pair))
    group = lax.axis_index("yhi")
    w_own = lax.dynamic_index_in_dim(w_here, group, 0, keepdims=False)
    w_other = lax.dynamic_index_in_dim(w_here, 1 - group, 0, keepdims=False)
    dims = (((1,), (1,)), ((), ()))
    part = lax.dot_general(h_own, w_own, dims, preferred_element_type=jnp.float32)
    part, far = lax.optimization_barrier((part, far))
    h_far = jnp.concatenate(far, axis=1)
    h_other = both_cores(h_far, lax.ppermute(h_far, "c", pair))
    part = part + lax.dot_general(h_other, w_other, dims, preferred_element_type=jnp.float32)
    part = part.astype(jnp.bfloat16).reshape(h_own.shape[0], -1)
    summed = lax.psum_scatter(part, "z", scatter_dimension=1, tiled=True)
    swapped = lax.all_to_all(summed, "c", split_axis=0, concat_axis=0, tiled=True)
    return jnp.concatenate([swapped[:tok_rows], swapped[tok_rows:]], axis=1)


def solution(mesh):
    seq_count, tp_count = mesh.devices.shape
    fine = Mesh(mesh.devices.reshape(2, seq_count // 4, 2, 2, tp_count // 2), SEQ + TP)
    in_specs = (P(SEQ, TP), P(SEQ, TP), P(SEQ, TP), P(), P(), P(TP, SEQ))
    out_specs = P(SEQ, TP)
    return jax.shard_map(
        functools.partial(shards, seq_count),
        mesh=fine,
        in_specs=in_specs,
        out_specs=out_specs,
        check_vma=False,
    )
```

```python
import functools
import math

import jax
import jax.numpy as jnp
from jax import lax
from jax.sharding import Mesh, PartitionSpec as P

HEAD_DIM = 128
WINDOW = 4096
BLOCK = 128
SEQ = ("ylo", "x", "c")
TP = ("yhi", "z")


def attend_head(q_rows, k_rows, v_rows, q_pos, k_pos, q_seg, k_seg):
    scores = lax.dot_general(
        q_rows, k_rows, (((1,), (1,)), ((), ())), preferred_element_type=jnp.float32
    )
    scores = scores * (1.0 / math.sqrt(HEAD_DIM))
    allowed = (k_pos[None, :] <= q_pos[:, None]) & (k_pos[None, :] > q_pos[:, None] - WINDOW)
    allowed = allowed & (k_seg[None, :] == q_seg[:, None])
    scores = jnp.where(allowed, scores, -jnp.inf)
    top_score = jnp.max(scores, axis=1, keepdims=True)
    expo = jnp.exp(scores - top_score)
    weights = (expo / jnp.sum(expo, axis=1, keepdims=True)).astype(jnp.bfloat16)
    return jnp.dot(weights, v_rows, preferred_element_type=jnp.float32).astype(jnp.bfloat16)


def shards(seq_count, queries, keys, values, segment_ids, packing, out_weight):
    tok_rows = queries.shape[0]
    q_cols = queries.shape[1]
    kv_cols = keys.shape[1]
    shard_index = lax.axis_index(SEQ)
    per_shard = tok_rows // BLOCK
    blocks_all = packing.shape[0]

    kv_local = jnp.concatenate([keys, values], axis=1)
    kv_all = lax.all_gather(kv_local, SEQ, axis=0, tiled=True)
    kv_blocks = kv_all.reshape(blocks_all, BLOCK, 2 * kv_cols)
    w_swapped = lax.ppermute(out_weight, ("ylo", "yhi"), perm=[(0, 0), (1, 2), (2, 1), (3, 3)])
    kv_blocks, w_swapped = lax.optimization_barrier((kv_blocks, w_swapped))
    w_here = lax.all_gather(w_swapped, ("ylo", "x"), axis=0, tiled=True)
    w_here = w_here.reshape(2, -1, out_weight.shape[0], out_weight.shape[1])

    target = packing[:, 0] * per_shard + packing[:, 1]
    source = jnp.zeros((blocks_all,), jnp.int32).at[target].set(
        jnp.arange(blocks_all, dtype=jnp.int32)
    )
    span_blocks = WINDOW // BLOCK
    ctx_blocks = span_blocks + per_shard
    blk_ids = shard_index * per_shard - span_blocks + jnp.arange(ctx_blocks, dtype=jnp.int32)
    src = jnp.take(source, jnp.clip(blk_ids, 0, blocks_all - 1))
    context = jnp.take(kv_blocks, src, axis=0).reshape(ctx_blocks * BLOCK, 2 * kv_cols)

    own_blocks = queries.reshape(per_shard, BLOCK, q_cols)
    own_list = lax.dynamic_slice_in_dim(packing, shard_index * per_shard, per_shard, 0)
    slot_ids = jnp.arange(seq_count, dtype=jnp.int32)
    routing = (own_list[:, 0][None, :] == slot_ids[:, None]).astype(jnp.bfloat16)
    outgoing = jnp.einsum(
        "db,brc->drc", routing, own_blocks, preferred_element_type=jnp.float32
    ).astype(jnp.bfloat16)
    incoming = lax.all_to_all(outgoing, SEQ, split_axis=0, concat_axis=0, tiled=True)
    arriving = packing[:, 0] == shard_index
    offset_ids = jnp.arange(per_shard, dtype=jnp.int32)
    at_offset = ((packing[:, 1][None, :] == offset_ids[:, None]) & arriving[None, :]).astype(
        jnp.float32
    )
    senders = jnp.arange(blocks_all, dtype=jnp.int32) // per_shard
    from_sender = (senders[:, None] == slot_ids[None, :]).astype(jnp.float32)
    placing = jnp.dot(at_offset, from_sender, precision=lax.Precision.HIGHEST).astype(jnp.bfloat16)
    packed = jnp.einsum(
        "od,drc->orc", placing, incoming, preferred_element_type=jnp.float32
    ).astype(jnp.bfloat16)
    queries_here = packed.reshape(tok_rows, q_cols)

    ctx_keys = context[:, :kv_cols]
    ctx_values = context[:, kv_cols:]
    ctx_rows = context.shape[0]
    q_pos = shard_index * tok_rows + jnp.arange(tok_rows, dtype=jnp.int32)
    k_pos = shard_index * tok_rows - WINDOW + jnp.arange(ctx_rows, dtype=jnp.int32)
    padded_seg = jnp.concatenate([jnp.full((WINDOW,), -1, jnp.int32), segment_ids], axis=0)
    q_seg = lax.dynamic_slice_in_dim(segment_ids, shard_index * tok_rows, tok_rows, 0)
    k_seg = lax.dynamic_slice_in_dim(padded_seg, shard_index * tok_rows, ctx_rows, 0)
    heads_here = q_cols // HEAD_DIM

    def one_head(head_index):
        q_head = lax.dynamic_slice_in_dim(queries_here, head_index * HEAD_DIM, HEAD_DIM, 1)
        return attend_head(q_head, ctx_keys, ctx_values, q_pos, k_pos, q_seg, k_seg)

    half = heads_here // 2
    pair = [(0, 1), (1, 0)]
    mine, far = [], []
    for first in (0, half):
        per_head = lax.map(one_head, jnp.arange(first, first + half, dtype=jnp.int32))
        piece = jnp.transpose(per_head, (1, 0, 2)).reshape(tok_rows, half * HEAD_DIM)
        mine.append(piece)
        far.append(lax.ppermute(piece, "yhi", pair))
    attended = jnp.concatenate(mine, axis=1)
    low_core = lax.axis_index("c") == 0

    def both_cores(here, there):
        return jnp.where(
            low_core,
            jnp.concatenate([here, there], axis=0),
            jnp.concatenate([there, here], axis=0),
        )

    h_own = both_cores(attended, lax.ppermute(attended, "c", pair))
    group = lax.axis_index("yhi")
    w_own = lax.dynamic_index_in_dim(w_here, group, 0, keepdims=False)
    w_other = lax.dynamic_index_in_dim(w_here, 1 - group, 0, keepdims=False)
    dims = (((1,), (1,)), ((), ()))
    part = lax.dot_general(h_own, w_own, dims, preferred_element_type=jnp.float32)
    part = part.astype(jnp.bfloat16)
    part, far = lax.optimization_barrier((part, far))
    h_far = jnp.concatenate(far, axis=1)
    h_other = both_cores(h_far, lax.ppermute(h_far, "c", pair))
    other = lax.dot_general(h_other, w_other, dims, preferred_element_type=jnp.float32)
    part = part.astype(jnp.float32) + other.astype(jnp.bfloat16).astype(jnp.float32)
    part = part.astype(jnp.bfloat16).reshape(h_own.shape[0], -1)
    summed = lax.psum_scatter(part, "z", scatter_dimension=1, tiled=True)
    swapped = lax.all_to_all(summed, "c", split_axis=0, concat_axis=0, tiled=True)
    return jnp.concatenate([swapped[:tok_rows], swapped[tok_rows:]], axis=1)


def solution(mesh):
    seq_count, tp_count = mesh.devices.shape
    fine = Mesh(mesh.devices.reshape(2, seq_count // 4, 2, 2, tp_count // 2), SEQ + TP)
    in_specs = (P(SEQ, TP), P(SEQ, TP), P(SEQ, TP), P(), P(), P(TP, SEQ))
    out_specs = P(SEQ, TP)
    return jax.shard_map(
        functools.partial(shards, seq_count),
        mesh=fine,
        in_specs=in_specs,
        out_specs=out_specs,
        check_vma=False,
    )
```

```python
import functools
import math

import jax
import jax.numpy as jnp
from jax import lax
from jax.sharding import Mesh, PartitionSpec as P

HEAD_DIM = 128
WINDOW = 4096
BLOCK = 128
SEQ = ("ylo", "x", "c")
TP = ("yhi", "z")


def attend_head(q_rows, k_rows, v_rows, q_pos, k_pos, q_seg, k_seg):
    scores = lax.dot_general(
        q_rows, k_rows, (((1,), (1,)), ((), ())), preferred_element_type=jnp.float32
    )
    scores = scores * (1.0 / math.sqrt(HEAD_DIM))
    allowed = (k_pos[None, :] <= q_pos[:, None]) & (k_pos[None, :] > q_pos[:, None] - WINDOW)
    allowed = allowed & (k_seg[None, :] == q_seg[:, None])
    scores = jnp.where(allowed, scores, -jnp.inf)
    top_score = jnp.max(scores, axis=1, keepdims=True)
    expo = jnp.exp(scores - top_score)
    weights = (expo / jnp.sum(expo, axis=1, keepdims=True)).astype(jnp.bfloat16)
    return jnp.dot(weights, v_rows, preferred_element_type=jnp.float32).astype(jnp.bfloat16)


def shards(seq_count, queries, keys, values, segment_ids, packing, out_weight):
    tok_rows = queries.shape[0]
    q_cols = queries.shape[1]
    kv_cols = keys.shape[1]
    shard_index = lax.axis_index(SEQ)
    per_shard = tok_rows // BLOCK
    blocks_all = packing.shape[0]

    kv_local = jnp.concatenate([keys, values], axis=1)
    kv_all = lax.all_gather(kv_local, SEQ, axis=0, tiled=True)
    kv_blocks = kv_all.reshape(blocks_all, BLOCK, 2 * kv_cols)
    w_swapped = lax.ppermute(out_weight, ("ylo", "yhi"), perm=[(0, 0), (1, 2), (2, 1), (3, 3)])
    kv_blocks, w_swapped = lax.optimization_barrier((kv_blocks, w_swapped))
    w_here = lax.all_gather(w_swapped, ("ylo", "x"), axis=0, tiled=True)
    w_here = w_here.reshape(2, -1, out_weight.shape[0], out_weight.shape[1])

    target = packing[:, 0] * per_shard + packing[:, 1]
    source = jnp.zeros((blocks_all,), jnp.int32).at[target].set(
        jnp.arange(blocks_all, dtype=jnp.int32)
    )
    span_blocks = WINDOW // BLOCK
    ctx_blocks = span_blocks + per_shard
    blk_ids = shard_index * per_shard - span_blocks + jnp.arange(ctx_blocks, dtype=jnp.int32)
    src = jnp.take(source, jnp.clip(blk_ids, 0, blocks_all - 1))
    context = jnp.take(kv_blocks, src, axis=0).reshape(ctx_blocks * BLOCK, 2 * kv_cols)

    own_blocks = queries.reshape(per_shard, BLOCK, q_cols)
    own_list = lax.dynamic_slice_in_dim(packing, shard_index * per_shard, per_shard, 0)
    slot_ids = jnp.arange(seq_count, dtype=jnp.int32)
    routing = (own_list[:, 0][None, :] == slot_ids[:, None]).astype(jnp.bfloat16)
    outgoing = jnp.einsum(
        "db,brc->drc", routing, own_blocks, preferred_element_type=jnp.float32
    ).astype(jnp.bfloat16)
    incoming = lax.all_to_all(outgoing, SEQ, split_axis=0, concat_axis=0, tiled=True)
    arriving = packing[:, 0] == shard_index
    offset_ids = jnp.arange(per_shard, dtype=jnp.int32)
    at_offset = ((packing[:, 1][None, :] == offset_ids[:, None]) & arriving[None, :]).astype(
        jnp.float32
    )
    senders = jnp.arange(blocks_all, dtype=jnp.int32) // per_shard
    from_sender = (senders[:, None] == slot_ids[None, :]).astype(jnp.float32)
    placing = jnp.dot(at_offset, from_sender, precision=lax.Precision.HIGHEST).astype(jnp.bfloat16)
    packed = jnp.einsum(
        "od,drc->orc", placing, incoming, preferred_element_type=jnp.float32
    ).astype(jnp.bfloat16)
    queries_here = packed.reshape(tok_rows, q_cols)

    ctx_keys = context[:, :kv_cols]
    ctx_values = context[:, kv_cols:]
    ctx_rows = context.shape[0]
    q_pos = shard_index * tok_rows + jnp.arange(tok_rows, dtype=jnp.int32)
    k_pos = shard_index * tok_rows - WINDOW + jnp.arange(ctx_rows, dtype=jnp.int32)
    padded_seg = jnp.concatenate([jnp.full((WINDOW,), -1, jnp.int32), segment_ids], axis=0)
    q_seg = lax.dynamic_slice_in_dim(segment_ids, shard_index * tok_rows, tok_rows, 0)
    k_seg = lax.dynamic_slice_in_dim(padded_seg, shard_index * tok_rows, ctx_rows, 0)
    heads_here = q_cols // HEAD_DIM

    def one_head(head_index):
        q_head = lax.dynamic_slice_in_dim(queries_here, head_index * HEAD_DIM, HEAD_DIM, 1)
        return attend_head(q_head, ctx_keys, ctx_values, q_pos, k_pos, q_seg, k_seg)

    half = heads_here // 3
    pair = [(0, 1), (1, 0)]
    mine, far = [], []
    for first in range(0, heads_here, half):
        per_head = lax.map(one_head, jnp.arange(first, first + half, dtype=jnp.int32))
        piece = jnp.transpose(per_head, (1, 0, 2)).reshape(tok_rows, half * HEAD_DIM)
        mine.append(piece)
        far.append(lax.ppermute(piece, "yhi", pair))
    attended = jnp.concatenate(mine, axis=1)
    h_far = jnp.concatenate(far, axis=1)
    low_hi = lax.axis_index("yhi") == 0
    h_groups = jnp.where(
        low_hi,
        jnp.concatenate([attended, h_far], axis=1),
        jnp.concatenate([h_far, attended], axis=1),
    )
    h_near = lax.ppermute(h_groups, "c", pair)
    low_core = lax.axis_index("c") == 0
    h_here = jnp.where(
        low_core,
        jnp.concatenate([h_groups, h_near], axis=0),
        jnp.concatenate([h_near, h_groups], axis=0),
    )
    h_split = h_here.reshape(h_here.shape[0], 2, -1)
    part = lax.dot_general(
        h_split, w_here, (((1, 2), (0, 2)), ((), ())), preferred_element_type=jnp.float32
    )
    part = part.astype(jnp.bfloat16).reshape(h_here.shape[0], -1)
    summed = lax.psum_scatter(part, "z", scatter_dimension=1, tiled=True)
    swapped = lax.all_to_all(summed, "c", split_axis=0, concat_axis=0, tiled=True)
    return jnp.concatenate([swapped[:tok_rows], swapped[tok_rows:]], axis=1)


def solution(mesh):
    seq_count, tp_count = mesh.devices.shape
    fine = Mesh(mesh.devices.reshape(2, seq_count // 4, 2, 2, tp_count // 2), SEQ + TP)
    in_specs = (P(SEQ, TP), P(SEQ, TP), P(SEQ, TP), P(), P(), P(TP, SEQ))
    out_specs = P(SEQ, TP)
    return jax.shard_map(
        functools.partial(shards, seq_count),
        mesh=fine,
        in_specs=in_specs,
        out_specs=out_specs,
        check_vma=False,
    )
```

```python
import functools
import math

import jax
import jax.numpy as jnp
from jax import lax
from jax.sharding import Mesh, PartitionSpec as P

HEAD_DIM = 128
WINDOW = 4096
BLOCK = 128
SEQ = ("ylo", "x", "c")
TP = ("yhi", "z")


def attend_head(q_rows, k_rows, v_rows, q_pos, k_pos, q_seg, k_seg):
    scores = lax.dot_general(
        q_rows, k_rows, (((1,), (1,)), ((), ())), preferred_element_type=jnp.float32
    )
    scores = scores * (1.0 / math.sqrt(HEAD_DIM))
    allowed = (k_pos[None, :] <= q_pos[:, None]) & (k_pos[None, :] > q_pos[:, None] - WINDOW)
    allowed = allowed & (k_seg[None, :] == q_seg[:, None])
    scores = jnp.where(allowed, scores, -jnp.inf)
    top_score = jnp.max(scores, axis=1, keepdims=True)
    expo = jnp.exp(scores - top_score)
    weights = (expo / jnp.sum(expo, axis=1, keepdims=True)).astype(jnp.bfloat16)
    return jnp.dot(weights, v_rows, preferred_element_type=jnp.float32).astype(jnp.bfloat16)


def shards(seq_count, queries, keys, values, segment_ids, packing, out_weight):
    tok_rows = queries.shape[0]
    q_cols = queries.shape[1]
    kv_cols = keys.shape[1]
    shard_index = lax.axis_index(SEQ)
    per_shard = tok_rows // BLOCK
    blocks_all = packing.shape[0]

    kv_local = jnp.concatenate([keys, values], axis=1)
    kv_all = lax.all_gather(kv_local, SEQ, axis=0, tiled=True)
    kv_blocks = kv_all.reshape(blocks_all, BLOCK, 2 * kv_cols)
    w_swapped = lax.ppermute(out_weight, ("ylo", "yhi"), perm=[(0, 0), (1, 2), (2, 1), (3, 3)])
    kv_blocks, w_swapped = lax.optimization_barrier((kv_blocks, w_swapped))
    w_here = lax.all_gather(w_swapped, ("ylo", "x"), axis=0, tiled=True)
    w_here = w_here.reshape(2, -1, out_weight.shape[0], out_weight.shape[1])

    target = packing[:, 0] * per_shard + packing[:, 1]
    source = jnp.zeros((blocks_all,), jnp.int32).at[target].set(
        jnp.arange(blocks_all, dtype=jnp.int32)
    )
    span_blocks = WINDOW // BLOCK
    ctx_blocks = span_blocks + per_shard
    blk_ids = shard_index * per_shard - span_blocks + jnp.arange(ctx_blocks, dtype=jnp.int32)
    src = jnp.take(source, jnp.clip(blk_ids, 0, blocks_all - 1))
    context = jnp.take(kv_blocks, src, axis=0).reshape(ctx_blocks * BLOCK, 2 * kv_cols)

    own_blocks = queries.reshape(per_shard, BLOCK, q_cols)
    own_list = lax.dynamic_slice_in_dim(packing, shard_index * per_shard, per_shard, 0)
    slot_ids = jnp.arange(seq_count, dtype=jnp.int32)
    routing = (own_list[:, 0][None, :] == slot_ids[:, None]).astype(jnp.bfloat16)
    outgoing = jnp.einsum(
        "db,brc->drc", routing, own_blocks, preferred_element_type=jnp.float32
    ).astype(jnp.bfloat16)
    incoming = lax.all_to_all(outgoing, SEQ, split_axis=0, concat_axis=0, tiled=True)
    arriving = packing[:, 0] == shard_index
    offset_ids = jnp.arange(per_shard, dtype=jnp.int32)
    at_offset = ((packing[:, 1][None, :] == offset_ids[:, None]) & arriving[None, :]).astype(
        jnp.float32
    )
    senders = jnp.arange(blocks_all, dtype=jnp.int32) // per_shard
    from_sender = (senders[:, None] == slot_ids[None, :]).astype(jnp.float32)
    placing = jnp.dot(at_offset, from_sender, precision=lax.Precision.HIGHEST).astype(jnp.bfloat16)
    packed = jnp.einsum(
        "od,drc->orc", placing, incoming, preferred_element_type=jnp.float32
    ).astype(jnp.bfloat16)
    queries_here = packed.reshape(tok_rows, q_cols)

    ctx_keys = context[:, :kv_cols]
    ctx_values = context[:, kv_cols:]
    ctx_rows = context.shape[0]
    q_pos = shard_index * tok_rows + jnp.arange(tok_rows, dtype=jnp.int32)
    k_pos = shard_index * tok_rows - WINDOW + jnp.arange(ctx_rows, dtype=jnp.int32)
    padded_seg = jnp.concatenate([jnp.full((WINDOW,), -1, jnp.int32), segment_ids], axis=0)
    q_seg = lax.dynamic_slice_in_dim(segment_ids, shard_index * tok_rows, tok_rows, 0)
    k_seg = lax.dynamic_slice_in_dim(padded_seg, shard_index * tok_rows, ctx_rows, 0)
    heads_here = q_cols // HEAD_DIM

    def one_head(head_index):
        q_head = lax.dynamic_slice_in_dim(queries_here, head_index * HEAD_DIM, HEAD_DIM, 1)
        return attend_head(q_head, ctx_keys, ctx_values, q_pos, k_pos, q_seg, k_seg)

    half = heads_here // 2
    pair = [(0, 1), (1, 0)]
    mine, far = [], []
    for first in (0, half):
        per_head = lax.map(one_head, jnp.arange(first, first + half, dtype=jnp.int32))
        piece = jnp.transpose(per_head, (1, 0, 2)).reshape(tok_rows, half * HEAD_DIM)
        mine.append(piece)
        far.append(lax.ppermute(piece, "yhi", pair))
    attended = jnp.concatenate(mine, axis=1)
    h_far = jnp.concatenate(far, axis=1)
    low_hi = lax.axis_index("yhi") == 0
    h_groups = jnp.where(
        low_hi,
        jnp.concatenate([attended, h_far], axis=1),
        jnp.concatenate([h_far, attended], axis=1),
    )
    h_near = lax.ppermute(h_groups, "c", pair)
    low_core = lax.axis_index("c") == 0
    h_here = jnp.where(
        low_core,
        jnp.concatenate([h_groups, h_near], axis=0),
        jnp.concatenate([h_near, h_groups], axis=0),
    )
    h_split = h_here.reshape(h_here.shape[0], 2, -1)
    part = lax.dot_general(
        h_split, w_here, (((1, 2), (0, 2)), ((), ())), preferred_element_type=jnp.float32
    )
    part = part.astype(jnp.bfloat16).reshape(h_here.shape[0], -1)
    summed = lax.psum_scatter(part, "z", scatter_dimension=1, tiled=True)
    kept = jnp.where(low_core, summed[:tok_rows], summed[tok_rows:])
    sent = jnp.where(low_core, summed[tok_rows:], summed[:tok_rows])
    got = lax.ppermute(sent, "c", pair)
    return jnp.where(
        low_core,
        jnp.concatenate([kept, got], axis=1),
        jnp.concatenate([got, kept], axis=1),
    )


def solution(mesh):
    seq_count, tp_count = mesh.devices.shape
    fine = Mesh(mesh.devices.reshape(2, seq_count // 4, 2, 2, tp_count // 2), SEQ + TP)
    in_specs = (P(SEQ, TP), P(SEQ, TP), P(SEQ, TP), P(), P(), P(TP, SEQ))
    out_specs = P(SEQ, TP)
    return jax.shard_map(
        functools.partial(shards, seq_count),
        mesh=fine,
        in_specs=in_specs,
        out_specs=out_specs,
        check_vma=False,
    )
```

```python
import functools
import math

import jax
import jax.numpy as jnp
from jax import lax
from jax.sharding import Mesh, PartitionSpec as P

HEAD_DIM = 128
WINDOW = 4096
BLOCK = 128
SEQ = ("ylo", "x", "c")
TP = ("yhi", "z")


def attend_head(q_rows, k_rows, v_rows, q_pos, k_pos, q_seg, k_seg):
    scores = lax.dot_general(
        q_rows, k_rows, (((1,), (1,)), ((), ())), preferred_element_type=jnp.float32
    )
    scores = scores * (1.0 / math.sqrt(HEAD_DIM))
    allowed = (k_pos[None, :] <= q_pos[:, None]) & (k_pos[None, :] > q_pos[:, None] - WINDOW)
    allowed = allowed & (k_seg[None, :] == q_seg[:, None])
    scores = jnp.where(allowed, scores, -jnp.inf)
    top_score = jnp.max(scores, axis=1, keepdims=True)
    expo = jnp.exp(scores - top_score)
    weights = (expo / jnp.sum(expo, axis=1, keepdims=True)).astype(jnp.bfloat16)
    return jnp.dot(weights, v_rows, preferred_element_type=jnp.float32).astype(jnp.bfloat16)


def shards(seq_count, queries, keys, values, segment_ids, packing, out_weight):
    tok_rows = queries.shape[0]
    q_cols = queries.shape[1]
    kv_cols = keys.shape[1]
    shard_index = lax.axis_index(SEQ)
    per_shard = tok_rows // BLOCK
    blocks_all = packing.shape[0]

    kv_local = jnp.concatenate([keys, values], axis=1)
    kv_all = lax.all_gather(kv_local, SEQ, axis=0, tiled=True)
    kv_blocks = kv_all.reshape(blocks_all, BLOCK, 2 * kv_cols)
    w_swapped = lax.ppermute(out_weight, ("ylo", "yhi"), perm=[(0, 0), (1, 2), (2, 1), (3, 3)])
    w_partner = lax.ppermute(w_swapped, "ylo", [(0, 1), (1, 0)])
    w_pair = jnp.where(
        lax.axis_index("ylo") == 0,
        jnp.stack([w_swapped, w_partner]),
        jnp.stack([w_partner, w_swapped]),
    )
    kv_blocks, w_pair = lax.optimization_barrier((kv_blocks, w_pair))
    w_here = lax.all_gather(w_pair, "x", axis=1, tiled=False)

    target = packing[:, 0] * per_shard + packing[:, 1]
    source = jnp.zeros((blocks_all,), jnp.int32).at[target].set(
        jnp.arange(blocks_all, dtype=jnp.int32)
    )
    span_blocks = WINDOW // BLOCK
    ctx_blocks = span_blocks + per_shard
    blk_ids = shard_index * per_shard - span_blocks + jnp.arange(ctx_blocks, dtype=jnp.int32)
    src = jnp.take(source, jnp.clip(blk_ids, 0, blocks_all - 1))
    context = jnp.take(kv_blocks, src, axis=0).reshape(ctx_blocks * BLOCK, 2 * kv_cols)

    own_blocks = queries.reshape(per_shard, BLOCK, q_cols)
    own_list = lax.dynamic_slice_in_dim(packing, shard_index * per_shard, per_shard, 0)
    slot_ids = jnp.arange(seq_count, dtype=jnp.int32)
    routing = (own_list[:, 0][None, :] == slot_ids[:, None]).astype(jnp.bfloat16)
    outgoing = jnp.einsum(
        "db,brc->drc", routing, own_blocks, preferred_element_type=jnp.float32
    ).astype(jnp.bfloat16)
    incoming = lax.all_to_all(outgoing, SEQ, split_axis=0, concat_axis=0, tiled=True)
    arriving = packing[:, 0] == shard_index
    offset_ids = jnp.arange(per_shard, dtype=jnp.int32)
    at_offset = ((packing[:, 1][None, :] == offset_ids[:, None]) & arriving[None, :]).astype(
        jnp.float32
    )
    senders = jnp.arange(blocks_all, dtype=jnp.int32) // per_shard
    from_sender = (senders[:, None] == slot_ids[None, :]).astype(jnp.float32)
    placing = jnp.dot(at_offset, from_sender, precision=lax.Precision.HIGHEST).astype(jnp.bfloat16)
    packed = jnp.einsum(
        "od,drc->orc", placing, incoming, preferred_element_type=jnp.float32
    ).astype(jnp.bfloat16)
    queries_here = packed.reshape(tok_rows, q_cols)

    ctx_keys = context[:, :kv_cols]
    ctx_values = context[:, kv_cols:]
    ctx_rows = context.shape[0]
    q_pos = shard_index * tok_rows + jnp.arange(tok_rows, dtype=jnp.int32)
    k_pos = shard_index * tok_rows - WINDOW + jnp.arange(ctx_rows, dtype=jnp.int32)
    padded_seg = jnp.concatenate([jnp.full((WINDOW,), -1, jnp.int32), segment_ids], axis=0)
    q_seg = lax.dynamic_slice_in_dim(segment_ids, shard_index * tok_rows, tok_rows, 0)
    k_seg = lax.dynamic_slice_in_dim(padded_seg, shard_index * tok_rows, ctx_rows, 0)
    heads_here = q_cols // HEAD_DIM

    def one_head(head_index):
        q_head = lax.dynamic_slice_in_dim(queries_here, head_index * HEAD_DIM, HEAD_DIM, 1)
        return attend_head(q_head, ctx_keys, ctx_values, q_pos, k_pos, q_seg, k_seg)

    half = heads_here // 2
    pair = [(0, 1), (1, 0)]
    mine, far = [], []
    for first in (0, half):
        per_head = lax.map(one_head, jnp.arange(first, first + half, dtype=jnp.int32))
        piece = jnp.transpose(per_head, (1, 0, 2)).reshape(tok_rows, half * HEAD_DIM)
        mine.append(piece)
        far.append(lax.ppermute(piece, "yhi", pair))
    attended = jnp.concatenate(mine, axis=1)
    h_far = jnp.concatenate(far, axis=1)
    low_hi = lax.axis_index("yhi") == 0
    h_groups = jnp.where(
        low_hi,
        jnp.concatenate([attended, h_far], axis=1),
        jnp.concatenate([h_far, attended], axis=1),
    )
    h_near = lax.ppermute(h_groups, "c", pair)
    low_core = lax.axis_index("c") == 0
    h_here = jnp.where(
        low_core,
        jnp.concatenate([h_groups, h_near], axis=0),
        jnp.concatenate([h_near, h_groups], axis=0),
    )
    h_split = h_here.reshape(h_here.shape[0], 2, -1)
    part = lax.dot_general(
        h_split, w_here, (((1, 2), (0, 2)), ((), ())), preferred_element_type=jnp.float32
    )
    part = part.astype(jnp.bfloat16).reshape(h_here.shape[0], -1)
    summed = lax.psum_scatter(part, "z", scatter_dimension=1, tiled=True)
    swapped = lax.all_to_all(summed, "c", split_axis=0, concat_axis=0, tiled=True)
    return jnp.concatenate([swapped[:tok_rows], swapped[tok_rows:]], axis=1)


def solution(mesh):
    seq_count, tp_count = mesh.devices.shape
    fine = Mesh(mesh.devices.reshape(2, seq_count // 4, 2, 2, tp_count // 2), SEQ + TP)
    in_specs = (P(SEQ, TP), P(SEQ, TP), P(SEQ, TP), P(), P(), P(TP, SEQ))
    out_specs = P(SEQ, TP)
    return jax.shard_map(
        functools.partial(shards, seq_count),
        mesh=fine,
        in_specs=in_specs,
        out_specs=out_specs,
        check_vma=False,
    )
```

```python
import functools
import math

import jax
import jax.numpy as jnp
from jax import lax
from jax.sharding import Mesh, PartitionSpec as P

HEAD_DIM = 128
WINDOW = 4096
BLOCK = 128
SEQ = ("ylo", "x", "c")
TP = ("yhi", "z")


def attend_head(q_rows, k_rows, v_rows, q_pos, k_pos, q_seg, k_seg):
    scores = lax.dot_general(
        q_rows, k_rows, (((1,), (1,)), ((), ())), preferred_element_type=jnp.float32
    )
    scores = scores * (1.0 / math.sqrt(HEAD_DIM))
    allowed = (k_pos[None, :] <= q_pos[:, None]) & (k_pos[None, :] > q_pos[:, None] - WINDOW)
    allowed = allowed & (k_seg[None, :] == q_seg[:, None])
    scores = jnp.where(allowed, scores, -jnp.inf)
    top_score = jnp.max(scores, axis=1, keepdims=True)
    expo = jnp.exp(scores - top_score)
    weights = (expo / jnp.sum(expo, axis=1, keepdims=True)).astype(jnp.bfloat16)
    return jnp.dot(weights, v_rows, preferred_element_type=jnp.float32).astype(jnp.bfloat16)


def shards(seq_count, queries, keys, values, segment_ids, packing, out_weight):
    tok_rows = queries.shape[0]
    q_cols = queries.shape[1]
    kv_cols = keys.shape[1]
    shard_index = lax.axis_index(SEQ)
    per_shard = tok_rows // BLOCK
    blocks_all = packing.shape[0]

    kv_local = jnp.concatenate([keys, values], axis=1)
    kv_all = lax.all_gather(kv_local, SEQ, axis=0, tiled=True)
    kv_blocks = kv_all.reshape(blocks_all, BLOCK, 2 * kv_cols)
    w_swapped = lax.ppermute(out_weight, ("ylo", "yhi"), perm=[(0, 0), (1, 2), (2, 1), (3, 3)])
    w_partner = lax.ppermute(w_swapped, "ylo", [(0, 1), (1, 0)])
    w_pair = jnp.where(
        lax.axis_index("ylo") == 0,
        jnp.stack([w_swapped, w_partner]),
        jnp.stack([w_partner, w_swapped]),
    )

    target = packing[:, 0] * per_shard + packing[:, 1]
    source = jnp.zeros((blocks_all,), jnp.int32).at[target].set(
        jnp.arange(blocks_all, dtype=jnp.int32)
    )
    span_blocks = WINDOW // BLOCK
    ctx_blocks = span_blocks + per_shard
    blk_ids = shard_index * per_shard - span_blocks + jnp.arange(ctx_blocks, dtype=jnp.int32)
    src = jnp.take(source, jnp.clip(blk_ids, 0, blocks_all - 1))
    context = jnp.take(kv_blocks, src, axis=0).reshape(ctx_blocks * BLOCK, 2 * kv_cols)

    own_blocks = queries.reshape(per_shard, BLOCK, q_cols)
    own_list = lax.dynamic_slice_in_dim(packing, shard_index * per_shard, per_shard, 0)
    slot_ids = jnp.arange(seq_count, dtype=jnp.int32)
    routing = (own_list[:, 0][None, :] == slot_ids[:, None]).astype(jnp.bfloat16)
    outgoing = jnp.einsum(
        "db,brc->drc", routing, own_blocks, preferred_element_type=jnp.float32
    ).astype(jnp.bfloat16)
    outgoing, w_pair = lax.optimization_barrier((outgoing, w_pair))
    w_here = lax.all_gather(w_pair, "x", axis=1, tiled=False)
    incoming = lax.all_to_all(outgoing, SEQ, split_axis=0, concat_axis=0, tiled=True)
    arriving = packing[:, 0] == shard_index
    offset_ids = jnp.arange(per_shard, dtype=jnp.int32)
    at_offset = ((packing[:, 1][None, :] == offset_ids[:, None]) & arriving[None, :]).astype(
        jnp.float32
    )
    senders = jnp.arange(blocks_all, dtype=jnp.int32) // per_shard
    from_sender = (senders[:, None] == slot_ids[None, :]).astype(jnp.float32)
    placing = jnp.dot(at_offset, from_sender, precision=lax.Precision.HIGHEST).astype(jnp.bfloat16)
    packed = jnp.einsum(
        "od,drc->orc", placing, incoming, preferred_element_type=jnp.float32
    ).astype(jnp.bfloat16)
    queries_here = packed.reshape(tok_rows, q_cols)

    ctx_keys = context[:, :kv_cols]
    ctx_values = context[:, kv_cols:]
    ctx_rows = context.shape[0]
    q_pos = shard_index * tok_rows + jnp.arange(tok_rows, dtype=jnp.int32)
    k_pos = shard_index * tok_rows - WINDOW + jnp.arange(ctx_rows, dtype=jnp.int32)
    padded_seg = jnp.concatenate([jnp.full((WINDOW,), -1, jnp.int32), segment_ids], axis=0)
    q_seg = lax.dynamic_slice_in_dim(segment_ids, shard_index * tok_rows, tok_rows, 0)
    k_seg = lax.dynamic_slice_in_dim(padded_seg, shard_index * tok_rows, ctx_rows, 0)
    heads_here = q_cols // HEAD_DIM

    def one_head(head_index):
        q_head = lax.dynamic_slice_in_dim(queries_here, head_index * HEAD_DIM, HEAD_DIM, 1)
        return attend_head(q_head, ctx_keys, ctx_values, q_pos, k_pos, q_seg, k_seg)

    half = heads_here // 2
    pair = [(0, 1), (1, 0)]
    mine, far = [], []
    for first in (0, half):
        per_head = lax.map(one_head, jnp.arange(first, first + half, dtype=jnp.int32))
        piece = jnp.transpose(per_head, (1, 0, 2)).reshape(tok_rows, half * HEAD_DIM)
        mine.append(piece)
        far.append(lax.ppermute(piece, "yhi", pair))
    attended = jnp.concatenate(mine, axis=1)
    h_far = jnp.concatenate(far, axis=1)
    low_hi = lax.axis_index("yhi") == 0
    h_groups = jnp.where(
        low_hi,
        jnp.concatenate([attended, h_far], axis=1),
        jnp.concatenate([h_far, attended], axis=1),
    )
    h_near = lax.ppermute(h_groups, "c", pair)
    low_core = lax.axis_index("c") == 0
    h_here = jnp.where(
        low_core,
        jnp.concatenate([h_groups, h_near], axis=0),
        jnp.concatenate([h_near, h_groups], axis=0),
    )
    h_split = h_here.reshape(h_here.shape[0], 2, -1)
    part = lax.dot_general(
        h_split, w_here, (((1, 2), (0, 2)), ((), ())), preferred_element_type=jnp.float32
    )
    part = part.astype(jnp.bfloat16).reshape(h_here.shape[0], -1)
    summed = lax.psum_scatter(part, "z", scatter_dimension=1, tiled=True)
    swapped = lax.all_to_all(summed, "c", split_axis=0, concat_axis=0, tiled=True)
    return jnp.concatenate([swapped[:tok_rows], swapped[tok_rows:]], axis=1)


def solution(mesh):
    seq_count, tp_count = mesh.devices.shape
    fine = Mesh(mesh.devices.reshape(2, seq_count // 4, 2, 2, tp_count // 2), SEQ + TP)
    in_specs = (P(SEQ, TP), P(SEQ, TP), P(SEQ, TP), P(), P(), P(TP, SEQ))
    out_specs = P(SEQ, TP)
    return jax.shard_map(
        functools.partial(shards, seq_count),
        mesh=fine,
        in_specs=in_specs,
        out_specs=out_specs,
        check_vma=False,
    )
```
